32 devices in a mesh: row: 4 (over y, x), col: 8 (over z, core).
Axes of the slice: x: 2, y: 2, z: 4, core: 2. Of those that a mesh axis runs over, the one named last changes fastest.
Arguments:
- image: bfloat16 [64, 256, 768], P('row', 'col'), may hold values from -6 to 6
- conv_taps: float32 [9, 768], replicated, may hold values from -0.5 to 0.5
- w_query: bfloat16 [768, 768], replicated, may hold values from -0.21875 to 0.21875
- w_key: bfloat16 [768, 768], replicated, may hold values from -0.21875 to 0.21875
- w_value: bfloat16 [768, 768], replicated, may hold values from -0.21875 to 0.21875
- w_out: bfloat16 [768, 768], replicated, may hold values from -0.21875 to 0.21875
- grad_out: bfloat16 [64, 256, 768], P('row', 'col'), may hold values from -6 to 6
Outputs:
- grad_image: bfloat16 [64, 256, 768], P('row', 'col')
- grad_weights: float32 [768, 3072], P(None, 'col')
- grad_conv: float32 [9, 768], P(None, 'col')
The draws below stay inside these ranges and needn't reach their ends.
All inputs are finite; a program needn't handle non-finite values.
Results may differ from the reference program's by a relative error of at most 0.022.
Values may be sent and summed in bfloat16 or wider, within the bound.
A program may use at most 128 MiB of HBM per device.

```python
import math
from functools import partial
import jax
import jax.numpy as jnp
from jax import lax

C = 768
HEADS = 12
HD = 64
POOL = 8
H = 64
W = 256
N_ROW = 4


def raised(drawn, own_key, source, target, blocks, factor):
    def block_of(axis_at):
        return (jnp.arange(drawn.shape[axis_at]) // (drawn.shape[axis_at] // blocks)).reshape((-1,) + (1,) * (drawn.ndim - 1 - axis_at))

    near = jax.random.permutation(own_key, blocks)[block_of(target)]
    second = (block_of(target) + blocks // 2) % blocks
    return jnp.where((block_of(source) == near) | (block_of(source) == second), factor * drawn, drawn)


def shard_levels(own_key, dims, cuts, smallest, largest):
    def one(dim, shards_of):
        steps = jax.random.uniform(jax.random.fold_in(jax.random.fold_in(own_key, 6), dim), (shards_of,), jnp.float32, smallest / len(cuts), largest / len(cuts))
        return jnp.repeat(jnp.exp(steps), dims[dim] // shards_of).reshape((-1,) + (1,) * (len(dims) - dim - 1))

    level = one(*cuts[0])
    for cut in cuts[1:]:
        level = level * one(*cut)
    return level


def noise(stream_key, shape, scale, reach, shards=(), kind=jnp.bfloat16):
    values = jax.random.normal(stream_key, shape, jnp.float32) * scale
    if len(shards) > 0:
        values = shard_levels(stream_key, shape, shards, -0.22, 0.18) * values
    return jnp.clip(values, min=-reach, max=reach).astype(kind)


def noise_with(key, shape, scale, reach, split, heavy, kind=jnp.bfloat16):
    values = scale * jax.random.normal(key, shape, jnp.float32)
    if split:
        values = values * shard_levels(key, shape, split, -0.22, 0.18)
    return jnp.clip(raised(values, jax.random.fold_in(key, 3), *heavy), -reach, reach).astype(kind)


def setup_inputs(seed: int = 0) -> dict:
    arg_keys = jax.random.split(jax.random.key(seed), 8)
    image = noise(arg_keys[0], (H, W, C), 1.0, 6.0, ((0, 4), (1, 8)))
    conv_taps = jnp.clip(jax.random.uniform(arg_keys[1], (9, C), jnp.float32, -0.5, 0.5), -0.5, 0.5)
    w_query = noise(arg_keys[2], (C, C), C ** -0.5, 0.21875)
    w_key = noise(arg_keys[3], (C, C), C ** -0.5, 0.21875)
    w_value = noise(arg_keys[4], (C, C), C ** -0.5, 0.21875)
    w_out = noise(arg_keys[5], (C, C), C ** -0.5, 0.21875)
    grad_out = noise_with(arg_keys[6], (H, W, C), 1.0, 6.0, ((0, 4), (1, 8)), (0, 2, 4, 2.0))
    return dict(image=image, conv_taps=conv_taps, w_query=w_query, w_key=w_key, w_value=w_value, w_out=w_out, grad_out=grad_out)


EPSILON = 1e-05

def contract_first(left, right):
    return lax.dot_general(left, right, (((0,), (0,)), ((), ())), preferred_element_type=jnp.float32)

def contract_last(left, right):
    return lax.dot_general(left, right, (((1,), (1,)), ((), ())), preferred_element_type=jnp.float32)

def exact_first(left, right):
    return lax.dot_general(left, right, (((0,), (0,)), ((), ())), precision=lax.Precision.HIGHEST, preferred_element_type=jnp.float32)

def exact_last(left, right):
    return lax.dot_general(left, right, (((1,), (1,)), ((), ())), precision=lax.Precision.HIGHEST, preferred_element_type=jnp.float32)

def stencil(padded, taps, height, width, flipped):
    total = jnp.zeros((height, width, padded.shape[2]), jnp.float32)
    for tap_row in range(3):
        for tap_col in range(3):
            if flipped:
                window = padded[2 - tap_row:2 - tap_row + height, 2 - tap_col:2 - tap_col + width]
            else:
                window = padded[tap_row:tap_row + height, tap_col:tap_col + width]
            total = total + taps[3 * tap_row + tap_col] * window.astype(jnp.float32)
    return total

def attend(carry, inputs, key_heads, value_heads):
    grad_key, grad_value = carry
    query_block, dout_block = inputs
    softmax_scale = HD ** (-0.5)
    query_heads = query_block.reshape(-1, HEADS, HD).astype(jnp.float32)
    dout_heads = dout_block.reshape(-1, HEADS, HD).astype(jnp.float32)
    key_float = key_heads.astype(jnp.float32)
    value_float = value_heads.astype(jnp.float32)
    scores = jnp.einsum('qhd,khd->hqk', query_heads, key_float) * softmax_scale
    expons = jnp.exp(scores)
    probabilities = expons / lax.optimization_barrier(jnp.sum(expons, axis=-1, keepdims=True))
    weights = probabilities.astype(jnp.bfloat16)
    attended = jnp.einsum('hqk,khd->qhd', weights.astype(jnp.float32), value_float).astype(jnp.bfloat16)
    grad_probs = jnp.einsum('qhd,khd->hqk', dout_heads, value_float)
    deltas = jnp.einsum('qhd,qhd->hq', dout_heads, attended.astype(jnp.float32))
    grad_scores = (probabilities * (grad_probs - deltas[:, :, None]) * softmax_scale).astype(jnp.bfloat16)
    grad_query = jnp.einsum('hqk,khd->qhd', grad_scores.astype(jnp.float32), key_float).astype(jnp.bfloat16)
    grad_key = grad_key + jnp.einsum('hqk,qhd->khd', grad_scores.astype(jnp.float32), query_heads)
    grad_value = grad_value + jnp.einsum('hqk,qhd->khd', weights.astype(jnp.float32), dout_heads)
    return ((grad_key, grad_value), (attended.reshape(query_block.shape), grad_query.reshape(query_block.shape)))

def reference(image, conv_taps, w_query, w_key, w_value, w_out, grad_out):
    height, width, channels = image.shape
    padded = jnp.pad(image, ((1, 1), (1, 1), (0, 0)))
    mixed = image.astype(jnp.float32) + stencil(padded, conv_taps, height, width, False)
    hidden = mixed.astype(jnp.bfloat16)
    flat_hidden = hidden.reshape(-1, channels)
    query = jnp.dot(flat_hidden, w_query, preferred_element_type=jnp.float32).astype(jnp.bfloat16)
    pooled = hidden.astype(jnp.float32).reshape(height // POOL, POOL, width // POOL, POOL, channels).mean(axis=(1, 3))
    centre = lax.optimization_barrier(jnp.mean(pooled, axis=-1, keepdims=True))
    spread = lax.optimization_barrier(jnp.mean(jnp.square(pooled - centre), axis=-1, keepdims=True))
    inverse = lax.rsqrt(spread + EPSILON)
    standard = (pooled - centre) * inverse
    normed = standard.astype(jnp.bfloat16)
    cells = normed.reshape(-1, channels)
    keys = jnp.dot(cells, w_key, preferred_element_type=jnp.float32).astype(jnp.bfloat16)
    values = jnp.dot(cells, w_value, preferred_element_type=jnp.float32).astype(jnp.bfloat16)
    flat_grad = grad_out.reshape(-1, channels)
    dout = contract_last(flat_grad, w_out).astype(jnp.bfloat16)
    row_queries = query.reshape(N_ROW, -1, channels)
    row_dout = dout.reshape(N_ROW, -1, channels)
    row_keys = keys.reshape(N_ROW, -1, HEADS, HD)
    row_values = values.reshape(N_ROW, -1, HEADS, HD)
    block_rows = math.gcd(row_queries.shape[1], 512)
    blocks = row_queries.shape[1] // block_rows

    def one_row(inputs):
        queries_row, dout_row, keys_row, values_row = inputs
        empty_grad = jnp.zeros(keys_row.shape, jnp.float32)
        carry, produced = lax.scan(partial(attend, key_heads=keys_row, value_heads=values_row), (empty_grad, empty_grad), (queries_row.reshape(blocks, block_rows, channels), dout_row.reshape(blocks, block_rows, channels)))
        return (carry[0], carry[1], produced[0].reshape(-1, channels), produced[1].reshape(-1, channels))
    grad_key, grad_value, attended, grad_query = lax.map(one_row, (row_queries, row_dout, row_keys, row_values))
    attended = attended.reshape(-1, channels)
    grad_query = grad_query.reshape(-1, channels)
    grad_key = grad_key.reshape(-1, channels)
    grad_value = grad_value.reshape(-1, channels)
    grad_wout = contract_first(attended, flat_grad)
    grad_wquery = contract_first(flat_hidden, grad_query)
    grad_hidden = contract_last(grad_query, w_query)
    cells_float = cells.astype(jnp.float32)
    grad_wkey = exact_first(cells_float, grad_key)
    grad_wvalue = exact_first(cells_float, grad_value)
    grad_normed = exact_last(grad_key, w_key.astype(jnp.float32)) + exact_last(grad_value, w_value.astype(jnp.float32))
    grad_normed = grad_normed.reshape(normed.shape)
    grad_pooled = (grad_normed - lax.optimization_barrier(jnp.mean(grad_normed, axis=-1, keepdims=True)) - standard * lax.optimization_barrier(jnp.mean(grad_normed * standard, axis=-1, keepdims=True))) * inverse
    pooled_rows, pooled_cols = (grad_pooled.shape[0], grad_pooled.shape[1])
    spread_back = jnp.broadcast_to((grad_pooled / (POOL * POOL))[:, None, :, None, :], (pooled_rows, POOL, pooled_cols, POOL, channels)).reshape(height, width, channels)
    grad_mixed = grad_out.astype(jnp.float32) + grad_hidden.reshape(height, width, channels) + spread_back
    grad_padded = jnp.pad(grad_mixed, ((1, 1), (1, 1), (0, 0)))
    grad_image = (grad_mixed + stencil(grad_padded, conv_taps, height, width, True)).astype(jnp.bfloat16)
    tap_list = []
    for tap_row in range(3):
        for tap_col in range(3):
            window = padded[tap_row:tap_row + height, tap_col:tap_col + width].astype(jnp.float32)
            tap_list.append(lax.optimization_barrier(jnp.sum(grad_mixed * window, axis=(0, 1))))
    grad_conv = jnp.stack(tap_list, axis=0)
    grad_weights = jnp.concatenate([grad_wquery, grad_wkey, grad_wvalue, grad_wout], axis=1)
    return (grad_image, grad_weights, grad_conv)
```

```python
from functools import partial
from types import SimpleNamespace

import jax
import jax.numpy as jnp
from jax import lax
from jax.experimental import pallas as pl
from jax.experimental.pallas import tpu as pltpu
from jax.sharding import PartitionSpec as P

HD = 64
POOL = 8
LANES = 128
WIDE = 256
EDGE = 16

EPSILON = 1e-05
LOG2E = 1.4426950408889634
MESH = pl.DeviceIdType.MESH
HBM = pl.BlockSpec(memory_space=pltpu.HBM)
DIRECTIONS = ((-1, -1), (-1, 1), (1, -1), (1, 1), (-1, 0), (1, 0), (0, -1), (0, 1))
CORNERS = (0, 1, 2, 3)
ROWS = (4, 5)
COLUMNS = (6, 7)
F32 = jnp.float32
BF16 = jnp.bfloat16


def contract(left, right, at_left, at_right):
    return lax.dot_general(
        left, right, (((at_left,), (at_right,)), ((), ())), preferred_element_type=F32
    )


def split(value):
    high = value.astype(BF16)
    return high, (value - high.astype(F32)).astype(BF16)


def remote(source, target, send, recv, row, col):
    return pltpu.make_async_remote_copy(
        src_ref=source,
        dst_ref=target,
        send_sem=send,
        recv_sem=recv,
        device_id=(row, col),
        device_id_type=MESH,
    )


def bits_of(count):
    return count.bit_length() - 1


def flip(row, bit):
    size = 2**bit
    return row + size * (1 - 2 * lax.rem(row // size, 2))


def block_kernel(rows_n, cols_n, names, *refs):
    r = SimpleNamespace(**dict(zip(names, refs, strict=True)))
    image, grad_out, taps = r.image_v, r.grad_out_v, r.taps_v
    pad1, pad2 = r.pad1, r.pad2
    hidden, query, dout = r.hidden, r.query, r.dout
    grad_query = r.grad_query
    height, width, channels = image.shape
    tokens = height * width
    own = (height // POOL) * (width // POOL)
    per_row = width // POOL
    cells_n = cols_n * own
    shard = 4 * channels // cols_n
    quarter = cols_n // 4
    half = quarter // 2
    groups = channels // WIDE
    part_lanes = shard // groups
    steps = bits_of(rows_n)
    parts = channels // LANES
    row, col = lax.axis_index("row"), lax.axis_index("col")
    chip, core = col // 2, lax.rem(col, 2)
    chips = cols_n // 2
    is_query = chip < half
    is_out = chip >= chips - half
    is_cells = jnp.logical_and(chip >= half, chip < chips - half)

    def row_mate(step):
        return lax.rem(row + step, rows_n)

    def col_mate(step):
        return lax.rem(col + step, cols_n)

    def row_partner(step):
        return (1 - core) * flip(row, step) + core * flip(row, steps - 1 - step)

    def position(of):
        def by(order):
            at = 0
            for step, bit in enumerate(order):
                size = 2**bit
                at = at + lax.rem(row // size + of // size, 2) * 2 ** (steps - 1 - step)
            return at

        return (1 - core) * by(range(steps)) + core * by(range(steps - 1, -1, -1))

    def present(down, right):
        ok = None
        for move, at, count in ((down, row, rows_n), (right, col, cols_n)):
            if move == 0:
                continue
            here = at > 0 if move < 0 else at < count - 1
            ok = here if ok is None else jnp.logical_and(ok, here)
        return ok

    def load(source, target, at):
        return pltpu.make_async_copy(source, target, r.loaded.at[at])

    load_image, load_taps = load(r.image, image, 0), load(r.taps, taps, 1)
    load_grad_out, load_out = load(r.grad_out, grad_out, 2), load(r.w_out, r.w_out_v, 3)
    load_query, load_key = load(r.w_query, r.w_query_v, 4), load(r.w_key, r.w_key_v, 5)
    load_value = load(r.w_value, r.w_value_v, 6)
    load_image.start()
    load_taps.start()

    halo1 = SimpleNamespace(
        pad=pad1, stage=r.stage1, side=r.side1, cols_out=r.cols_out1, cols_in=r.cols_in1, rows_in=r.rows_in1,
        corners_out=r.corners_out1, corners_in=r.corners_in1, send=r.halo_send1, recv=r.halo_recv1,
        edge_rows=(r.image.at[0], r.image.at[height - 1]),
    )
    halo2 = SimpleNamespace(
        pad=pad2, stage=r.stage2, side=r.side2, cols_out=r.cols_out2, cols_in=r.cols_in2, rows_in=r.rows_in2,
        corners_out=r.corners_out2, corners_in=r.corners_in2, send=r.halo_send2, recv=r.halo_recv2,
        edge_rows=(r.rows_out2.at[0], r.rows_out2.at[1]),
    )
    for halo in (halo1, halo2):
        for ref in (halo.cols_in, halo.rows_in, halo.corners_in):
            ref[...] = jnp.zeros_like(ref)

    barrier = pltpu.get_barrier_semaphore()
    greeted = cols_n + rows_n - 2
    for down, right in DIRECTIONS[:4]:
        greeted = greeted + present(down, right).astype(jnp.int32)

        @pl.when(present(down, right))
        def _(down=down, right=right):
            pl.semaphore_signal(barrier, inc=1, device_id=(row + down, col + right), device_id_type=MESH)
    for step in range(1, cols_n):
        pl.semaphore_signal(barrier, inc=1, device_id=(row, col_mate(step)), device_id_type=MESH)
    for step in range(1, rows_n):
        pl.semaphore_signal(barrier, inc=1, device_id=(row_mate(step), col), device_id_type=MESH)

    def edge(halo, at):
        down, right = DIRECTIONS[at]
        edge_row = halo.edge_rows[0 if down < 0 else 1]
        if down == 0:
            source, target = halo.cols_out.at[0 if right < 0 else 1], halo.cols_in.at[1 if right < 0 else 0]
        elif right == 0:
            source, target = edge_row, halo.rows_in.at[1 if down < 0 else 0]
        else:
            source = halo.corners_out.at[(0 if down < 0 else 2) + (0 if right < 0 else 1), pl.ds(0, 1)]
            target = halo.corners_in.at[(2 if down < 0 else 0) + (1 if right < 0 else 0), pl.ds(0, 1)]
        return remote(source, target, halo.send.at[at], halo.recv.at[at], row + down, col + right)

    def pack_edges(halo, first, last):
        for at in range(height):
            for which, value in enumerate((first(at), last(at))):
                halo.stage[which, at : at + 1] = value
                if at == 0 or at == height - 1:
                    halo.corners_out[(0 if at == 0 else 2) + which, 0:1] = value
        halo.cols_out[...] = halo.stage[...].astype(BF16)

    def send_halo(halo, wanted):
        for at in wanted:
            down, right = DIRECTIONS[at]

            @pl.when(present(down, right))
            def _(at=at):
                edge(halo, at).start()

    def wait_halo(halo):
        for at, (down, right) in enumerate(DIRECTIONS):
            @pl.when(present(-down, -right))
            def _(at=at):
                edge(halo, at).wait_recv()

            @pl.when(present(down, right))
            def _(at=at):
                edge(halo, at).wait_send()

    def take_halo(halo):
        halo.pad[0] = halo.rows_in[0].astype(F32)
        halo.pad[height + 1] = halo.rows_in[1].astype(F32)
        for which in range(2):
            halo.side[which, 1 : height + 1] = halo.cols_in[which].astype(F32)
            halo.side[which, 0:1] = halo.corners_in[which, 0:1]
            halo.side[which, height + 1 : height + 2] = halo.corners_in[2 + which, 0:1]

    sublane = lax.broadcasted_iota(jnp.int32, (width, LANES), 0)
    first_column, last_column = sublane == 0, sublane == width - 1

    def from_left(value, halo):
        return jnp.where(first_column, halo, pltpu.roll(value, 1, 0))

    def from_right(value, halo):
        return jnp.where(last_column, halo, pltpu.roll(value, width - 1, 0))

    def lanes_of(part):
        return pl.ds(pl.multiple_of(part * LANES, LANES), LANES)

    pl.semaphore_wait(barrier, greeted)
    send_halo(halo1, ROWS)
    load_image.wait()
    for copy in (load_grad_out, load_out, load_query, load_key, load_value):
        copy.start()
    pack_edges(
        halo1,
        lambda at: image[at, :EDGE].astype(F32)[:1],
        lambda at: image[at, width - EDGE :].astype(F32)[EDGE - 1 :],
    )
    send_halo(halo1, CORNERS + COLUMNS)
    load_taps.wait()
    pad1[0] = jnp.zeros_like(pad1[0])
    pad1[height + 1] = jnp.zeros_like(pad1[0])

    @pl.loop(0, height)
    def _(at):
        pad1[at + 1] = image[at].astype(F32)

    def weights_of(lanes):
        w = [jnp.broadcast_to(taps[i : i + 1, lanes], (width, LANES)) for i in range(9)]
        w[4] = w[4] + 1.0
        return w

    @pl.loop(0, parts)
    def _(part):
        lanes = lanes_of(part)
        w = weights_of(lanes)
        for at in range(height):
            x = [pad1[at + a, :, lanes] for a in range(3)]
            sums = [w[b] * x[0] + w[3 + b] * x[1] + w[6 + b] * x[2] for b in range(3)]
            r.mixed[at, :, lanes] = sums[1] + from_left(sums[0], 0.0) + from_right(sums[2], 0.0)

    chunk = tokens // 2

    def chunk_of(at):
        return pl.ds(pl.multiple_of(at * chunk, chunk), chunk)

    load_grad_out.wait()
    load_out.wait()

    @pl.loop(0, 2)
    def _(at):
        rows = chunk_of(at)
        dout[rows] = contract(grad_out[rows], r.w_out_v[...], 1, 1).astype(BF16)

    for side in range(2):
        for item in range(half):
            at = (2 * item + side) * shard
            r.go_split[side, item] = grad_out[:, at : at + shard]

    def to_mate(source, target, at):
        return remote(source, target, r.mate_send.at[at], r.mate_recv.at[at], row, 2 * chip + 1 - core)

    go_copy = to_mate(r.go_split.at[1 - core], r.go_in, 0)
    go_copy.start()
    wait_halo(halo1)
    take_halo(halo1)

    edge_sublane = lax.broadcasted_iota(jnp.int32, (8, LANES), 0)

    @pl.loop(0, parts)
    def _(part):
        lanes = lanes_of(part)
        w = [jnp.broadcast_to(taps[i : i + 1, lanes], (width, LANES)) for i in range(9)]
        short = [jnp.broadcast_to(taps[i : i + 1, lanes], (height, LANES)) for i in range(9)]
        for which in range(2):
            total = jnp.zeros((height, LANES), F32)
            for a in range(3):
                total = total + short[3 * a + 2 * which] * r.side1[which, a : a + height, lanes]
            r.edge_sum[which, :, lanes] = total
        for cell_row in range(height // POOL):
            pooled = jnp.zeros((width, LANES), F32)
            for at in range(cell_row * POOL, (cell_row + 1) * POOL):
                total = r.mixed[at, :, lanes]
                for edge_at, a in ((0, 0), (height - 1, 2)):
                    if at == edge_at:
                        x = pad1[at + a, :, lanes]
                        total = (
                            total + w[3 * a + 1] * x + from_left(w[3 * a] * x, 0.0) + from_right(w[3 * a + 2] * x, 0.0)
                        )
                left = jnp.where(edge_sublane == 0, r.edge_sum[0, at : at + 1, lanes], 0.0)
                right = jnp.where(edge_sublane == 7, r.edge_sum[1, at : at + 1, lanes], 0.0)
                total = jnp.concatenate(
                    [total[:8] + left, total[8 : width - 8], total[width - 8 :] + right], axis=0
                )
                value = total.astype(BF16)
                hidden[at * width : (at + 1) * width, lanes] = value
                pooled = pooled + value.astype(F32)
            where = slice(cell_row * per_row, (cell_row + 1) * per_row)
            r.pooled[where, lanes] = pooled.reshape(per_row, POOL, LANES).sum(axis=1) / (POOL * POOL)

    pooled = r.pooled[...]
    centre = jnp.mean(pooled, axis=-1, keepdims=True)
    spread = jnp.mean(jnp.square(pooled - centre), axis=-1, keepdims=True)
    inverse = lax.rsqrt(spread + EPSILON)
    standard = (pooled - centre) * inverse
    cellbuf = r.cellbuf
    cellbuf[col] = standard.astype(BF16)

    def cell(step):
        return remote(
            cellbuf.at[col], cellbuf.at[col], r.cell_send.at[step - 1], r.cell_recv.at[step - 1], row, col_mate(step)
        )

    for step in range(1, cols_n):
        cell(step).start()
    hidden_copy = to_mate(hidden, r.hidden_in, 1)
    hidden_copy.start()

    load_query.wait()

    @pl.loop(0, 2)
    def _(at):
        rows = chunk_of(at)
        query[rows] = contract(hidden[rows], r.w_query_v[...], 1, 0).astype(BF16)

    @pl.loop(0, parts)
    def _(part):
        lanes = lanes_of(part)
        for cell_row in range(height // POOL):
            for a in range(3):
                first = cell_row * POOL + a
                total = pad1[first, :, lanes]
                for at in range(first + 1, first + POOL):
                    total = total + pad1[at, :, lanes]
                left, right = (
                    r.side1[which, first : first + POOL, lanes].sum(axis=0, keepdims=True) for which in range(2)
                )
                for b, value in enumerate((from_left(total, left), total, from_right(total, right))):
                    r.windows[3 * a + b, cell_row * per_row : (cell_row + 1) * per_row, lanes] = value.reshape(
                        per_row, POOL, LANES
                    ).sum(axis=1)

    load_key.wait()
    load_value.wait()
    for step in range(1, cols_n):
        cell(step).wait()
    key_cells = jnp.concatenate([cellbuf[at].astype(F32) for at in range(cols_n)], axis=0).astype(BF16)
    r.key_all[row] = key_cells

    def pass_on(ref, at, step):
        return remote(
            ref.at[row], ref.at[row], r.pass_send.at[at, step - 1], r.pass_recv.at[at, step - 1], row_mate(step), col
        )

    @pl.when(is_cells)
    def _():
        for step in range(1, rows_n):
            pass_on(r.key_all, 0, step).start()

    r.keys[...] = contract(key_cells, r.w_key_v[...], 1, 0).astype(BF16)
    r.values[...] = contract(key_cells, r.w_value_v[...], 1, 0).astype(BF16)

    heads = WIDE // HD
    wide_cells = heads * cells_n
    same_head = (
        lax.broadcasted_iota(jnp.int32, (wide_cells, WIDE), 0) // cells_n
        == lax.broadcasted_iota(jnp.int32, (wide_cells, WIDE), 1) // HD
    )
    cell_ones = (
        lax.broadcasted_iota(jnp.int32, (wide_cells, wide_cells), 0) // cells_n
        == lax.broadcasted_iota(jnp.int32, (wide_cells, wide_cells), 1) // cells_n
    ).astype(F32).astype(BF16)
    scale = HD ** (-0.5)
    lane_ones = (
        (
            lax.broadcasted_iota(jnp.int32, (WIDE, wide_cells), 0) // HD
            == lax.broadcasted_iota(jnp.int32, (WIDE, wide_cells), 1) // cells_n
        ).astype(F32) * scale
    ).astype(BF16)
    head_of = lax.broadcasted_iota(jnp.int32, (cells_n, WIDE), 1) // HD
    places = [[(k * shard + g * part_lanes, k) for k in range(quarter)] for g in range(groups)]

    def take(ref, g):
        return jnp.concatenate([ref[:, at : at + part_lanes] for at, _ in places[g]], axis=1)

    def by_head(value):
        total = value[:cells_n]
        for head in range(1, heads):
            total = jnp.where(head_of == head, value[head * cells_n : (head + 1) * cells_n], total)
        return total

    def attend(g):
        def both(ref, factor):
            value = take(ref, g).astype(F32) * factor
            return jnp.where(same_head, jnp.concatenate([value] * heads, axis=0), 0.0).astype(BF16)

        key_wide, value_wide, value_scaled = both(r.keys, 1.0), both(r.values, 1.0), both(r.values, scale)
        queries, douts = take(query, g), take(dout, g)
        expons = jnp.exp2(contract(queries, key_wide, 1, 1) * (scale * LOG2E))
        sums = contract(expons.astype(BF16), cell_ones, 1, 0)
        probabilities = expons / sums
        weights = probabilities.astype(BF16)
        got = contract(weights, value_wide, 1, 0).astype(BF16)
        r.att[g] = got
        grad_probs = contract(douts, value_scaled, 1, 1)
        deltas = contract((douts.astype(F32) * got.astype(F32)).astype(BF16), lane_ones, 1, 0)
        grad_scores = (probabilities * (grad_probs - deltas)).astype(BF16)
        grad_queries = contract(grad_scores, key_wide, 1, 0).astype(BF16)
        for at, k in places[g]:
            piece = grad_queries[:, k * part_lanes : (k + 1) * part_lanes]
            grad_query[:, at : at + part_lanes] = piece
            r.gq_split[g, k % 2, k // 2] = piece
        to_mate(r.gq_split.at[g, 1 - core], r.gq_in.at[g], 2 + g).start()
        to_mate(r.att.at[g], r.att_in.at[g], 2 + groups + g).start()
        grad_key = by_head(contract(grad_scores, queries, 0, 0))
        grad_value = by_head(contract(weights, douts, 0, 0))
        for owner in range(cols_n):
            rows = slice(owner * own, (owner + 1) * own)
            both_rows = jnp.concatenate([grad_key[rows], grad_value[rows]], axis=0).astype(BF16)
            for at, k in places[g]:
                r.blocks[owner, :, at : at + part_lanes] = both_rows[:, k * part_lanes : (k + 1) * part_lanes]

    def block(step):
        owner = col_mate(step)
        return remote(
            r.blocks.at[owner], r.blocks_in.at[step - 1], r.block_send.at[step - 1], r.block_recv.at[step - 1], row, owner
        )

    KINDS = (0, 1)
    made = (r.terms_q, r.terms_o)
    landed = (r.landed_q, r.landed_o)
    held = (r.held_q, r.held_o)
    line = (r.line_q, r.line_o)
    fin = (r.fin_q, r.fin_o)

    def terms(g):
        to_mate(r.gq_split.at[g, 1 - core], r.gq_in.at[g], 2 + g).wait()
        to_mate(r.att.at[g], r.att_in.at[g], 2 + groups + g).wait()
        for item in range(half):
            for_query = contract(hidden[...], r.gq_split[g, core, item], 0, 0) + contract(
                r.hidden_in[...], r.gq_in[g, item], 0, 0
            )
            for_out = contract(r.att[g], r.go_split[core, item], 0, 0) + contract(
                r.att_in[g], r.go_in[item], 0, 0
            )
            for kind, value in enumerate((for_query, for_out)):
                value = value.astype(BF16)
                size = value.shape[0] // rows_n
                for at in range(rows_n):
                    made[kind][g, item, position(at)] = value[at * size : (at + 1) * size]

    def halving(g, kind, item, step):
        count = rows_n >> (step + 1)
        base = made[kind] if step == 0 else held[kind]
        offset = rows_n - 2 * count
        number = kind * half + item
        return remote(
            base.at[g, item, pl.ds(count, count)], landed[kind].at[g, item, pl.ds(offset, count)],
            r.half_send.at[g, number, step], r.half_recv.at[g, number, step], row_partner(step), col,
        )

    def halve_start(g, step):
        for kind in KINDS:
            for item in range(half):
                halving(g, kind, item, step).start()

    def halve_finish(g, step):
        count = rows_n >> (step + 1)
        offset = rows_n - 2 * count
        for kind in KINDS:
            for item in range(half):
                halving(g, kind, item, step).wait()
                base = made[kind] if step == 0 else held[kind]
                held[kind][g, item, 0:count] = (
                    base[g, item, 0:count].astype(F32)
                    + landed[kind][g, item, offset : offset + count].astype(F32)
                ).astype(BF16)
                if step < steps - 1:
                    halving(g, kind, item, step + 1).start()
                else:
                    @pl.when(chip != owner_of(kind, item))
                    def _(kind=kind, item=item):
                        along(g, kind, item).start()

    def owner_of(kind, item):
        return item if kind == 0 else chips - half + item

    def along(g, kind, item):
        number = kind * half + item
        return remote(
            held[kind].at[g, item, 0], line[kind].at[g, chip],
            r.line_send.at[g, number], r.line_recv.at[g, chip], row, 2 * owner_of(kind, item) + core,
        )

    def arrived(g, kind, source):
        return remote(
            held[kind].at[g, 0, 0], line[kind].at[g, source],
            r.line_send.at[g, 0], r.line_recv.at[g, source], row, 2 * source + core,
        )

    def spread_out(g, kind, step):
        return remote(
            fin[kind].at[g, row], fin[kind].at[g, row],
            r.spread_send.at[g, step - 1], r.spread_recv.at[g, step - 1], row_mate(step), col,
        )

    def each_owner(body):
        for kind, here, item in ((0, is_query, chip), (1, is_out, chip - (chips - half))):
            @pl.when(here)
            def _(kind=kind, item=item):
                body(kind, item)

    def line_finish(g):
        def body(kind, item):
            total = held[kind][g, item, 0].astype(F32)
            for step in range(1, chips):
                source = lax.rem(chip + step, chips)
                arrived(g, kind, source).wait_recv()
                total = total + line[kind][g, source].astype(F32)
            fin[kind][g, row] = total.astype(BF16)
            for step in range(1, rows_n):
                spread_out(g, kind, step).start()

        each_owner(body)

    def place_final(g):
        def body(kind, item):
            for step in range(1, rows_n):
                spread_out(g, kind, step).wait()
            for part in range(rows_n):
                value = fin[kind][g, part].astype(F32)
                if kind == 0:
                    size = channels // rows_n
                    r.grad_weights[part * size : (part + 1) * size, g * part_lanes : (g + 1) * part_lanes] = value
                else:
                    size = WIDE // rows_n
                    k = (part * size) // part_lanes
                    at = k * shard + g * part_lanes + part * size - k * part_lanes
                    r.grad_weights[at : at + size] = value

        each_owner(body)

    go_copy.wait()
    hidden_copy.wait()
    attend(0)
    for g in range(1, groups):
        attend(g)
        if g == groups - 1:
            for step in range(1, cols_n):
                block(step).start()
        terms(g - 1)
        halve_start(g - 1, 0)
    terms(groups - 1)
    halve_start(groups - 1, 0)

    @pl.loop(0, 2)
    def _(at):
        rows = chunk_of(at)
        value = contract(grad_query[rows], r.w_query_v[...], 1, 1) + grad_out[rows].astype(F32)
        pad2[pl.ds(1 + at * (height // 2), height // 2)] = value.reshape(height // 2, width, channels)

    halve_finish(0, 0)

    for at in range(height):
        for which, value in enumerate((pad2[at + 1, 0:1], pad2[at + 1, width - 1 : width])):
            r.stage1[which, at : at + 1] = value
    r.tap_terms[...] = jnp.zeros_like(r.tap_terms)

    @pl.loop(0, parts)
    def _(part):
        lanes = lanes_of(part)
        sums = [jnp.zeros((8, LANES), F32) for _ in range(9)]
        for at in range(height):
            value = pad2[at + 1, :, lanes]
            shifted = [from_right(value, 0.0), value, from_left(value, 0.0)]
            for a in range(3):
                x = pad1[at + a, :, lanes]
                for b in range(3):
                    sums[3 * a + b] = sums[3 * a + b] + (shifted[b] * x).reshape(width // 8, 8, LANES).sum(axis=0)
        for i in range(9):
            total = sums[i].sum(axis=0, keepdims=True)
            if i % 3 != 1:
                which = 0 if i % 3 == 0 else 1
                product = r.stage1[which, :, lanes] * r.side1[which, i // 3 : i // 3 + height, lanes]
                total = total + product.sum(axis=0, keepdims=True)
            r.tap_terms[i : i + 1, lanes] = total

    totals = r.blocks[col].astype(F32)
    for step in range(1, cols_n):
        block(step).wait()
        totals = totals + r.blocks_in[step - 1].astype(F32)
    high, low = split(totals)
    tot_all = r.tot_all
    tot_all[col] = high

    def tot(target):
        return remote(
            tot_all.at[col], tot_all.at[col], r.tot_send.at[target - quarter], r.tot_recv.at[col], row, target
        )

    def tot_from(source):
        return remote(
            tot_all.at[source], tot_all.at[source], r.tot_send.at[0], r.tot_recv.at[source], row, source
        )

    for target in range(quarter, 3 * quarter):
        @pl.when(col != target)
        def _(target=target):
            tot(target).start()

    both_parts = jnp.concatenate([high, low], axis=0)
    by_key = contract(both_parts, r.w_key_v[...], 1, 1)
    by_value = contract(both_parts, r.w_value_v[...], 1, 1)
    grad_normed = by_key[:own] + by_key[2 * own : 3 * own] + by_value[own : 2 * own] + by_value[3 * own :]
    grad_pooled = (
        grad_normed
        - jnp.mean(grad_normed, axis=-1, keepdims=True)
        - standard * jnp.mean(grad_normed * standard, axis=-1, keepdims=True)
    ) * (inverse / (POOL * POOL))
    r.grad_pooled[...] = grad_pooled
    tap_out, tap_in, tap_out2, tap_in2 = r.tap_out, r.tap_in, r.tap_out2, r.tap_in2
    for i in range(9):
        r.tap_terms[i : i + 1] = r.tap_terms[i : i + 1] + (r.windows[i] * grad_pooled).sum(axis=0, keepdims=True)
    tap_out[...] = r.tap_terms[...].astype(BF16)

    def tap_first(step):
        return remote(tap_out, tap_in.at[step - 1], r.tap_send1.at[step - 1], r.tap_recv1.at[step - 1], row_mate(step), col)

    def tap_second(step):
        return remote(tap_out2, tap_in2.at[step - 1], r.tap_send2.at[step - 1], r.tap_recv2.at[step - 1], row, col_mate(step))

    for step in range(1, rows_n):
        tap_first(step).start()

    halve_finish(1, 0)

    @pl.loop(0, parts)
    def _(part):
        lanes = lanes_of(part)
        for cell_row in range(height // POOL):
            over = jnp.concatenate(
                [
                    jnp.broadcast_to(r.grad_pooled[at : at + 1, lanes], (POOL, LANES))
                    for at in range(cell_row * per_row, (cell_row + 1) * per_row)
                ],
                axis=0,
            )
            for at in range(cell_row * POOL, (cell_row + 1) * POOL):
                value = pad2[at + 1, :, lanes] + over
                pad2[at + 1, :, lanes] = value
                if at == 0 or at == height - 1:
                    r.rows_out2[0 if at == 0 else 1, :, lanes] = value.astype(BF16)

    pack_edges(halo2, lambda at: pad2[at + 1, 0:1], lambda at: pad2[at + 1, width - 1 : width])
    send_halo(halo2, range(8))

    for step in range(1, steps):
        halve_finish(0, step)
    for g in range(2, groups):
        halve_finish(g, 0)
    for g in range(1, groups - 1):
        for step in range(1, steps):
            halve_finish(g, step)

    @pl.when(is_cells)
    def _():
        for step in range(1, cols_n):
            tot_from(col_mate(step)).wait_recv()
        is_key = col < 2 * quarter
        sides = []
        for at in range(cols_n):
            value = tot_all[at].astype(F32)
            sides.append(jnp.where(is_key, value[:own], value[own:]))
        value = jnp.concatenate(sides, axis=0)
        mine = value[:, :shard]
        for k in range(1, quarter):
            mine = jnp.where(lax.rem(col, quarter) == k, value[:, k * shard : (k + 1) * shard], mine)
        r.side_all[row] = mine.astype(BF16)
        for step in range(1, rows_n):
            pass_on(r.side_all, 1, step).start()

    tap_total = tap_out[...].astype(F32)
    for step in range(1, rows_n):
        tap_first(step).wait()
        tap_total = tap_total + tap_in[step - 1].astype(F32)
    tap_out2[...] = tap_total.astype(BF16)
    for step in range(1, cols_n):
        tap_second(step).start()

    for step in range(1, steps):
        halve_finish(groups - 1, step)
    wait_halo(halo2)
    take_halo(halo2)

    @pl.loop(0, parts)
    def _(part):
        lanes = lanes_of(part)
        w = weights_of(lanes)
        short = [jnp.broadcast_to(taps[i : i + 1, lanes], (height, LANES)) for i in range(9)]
        for which in range(2):
            total = jnp.zeros((height, LANES), F32)
            for a in range(3):
                total = total + short[3 * a + 2 - 2 * which] * r.side2[which, 2 - a : 2 - a + height, lanes]
            r.edge_sum[which, :, lanes] = total
        for at in range(height):
            x = [pad2[at + 2 - a, :, lanes] for a in range(3)]
            sums = [w[b] * x[0] + w[3 + b] * x[1] + w[6 + b] * x[2] for b in range(3)]
            total = (
                sums[1]
                + from_right(sums[0], r.edge_sum[1, at : at + 1, lanes])
                + from_left(sums[2], r.edge_sum[0, at : at + 1, lanes])
            )
            r.grad_image[at, :, lanes] = total.astype(BF16)

    line_finish(0)

    @pl.when(is_cells)
    def _():
        for at, ref in enumerate((r.key_all, r.side_all)):
            for step in range(1, rows_n):
                pass_on(ref, at, step).wait()
        keys = r.key_all[...].reshape(rows_n * cells_n, channels)
        sides = r.side_all[...].reshape(rows_n * cells_n, shard)
        r.grad_weights[...] = contract(keys, sides, 0, 0)

    for g in range(1, groups - 1):
        line_finish(g)

    tap_total = tap_out2[...].astype(F32)
    for step in range(1, cols_n):
        tap_second(step).wait()
        tap_total = tap_total + tap_in2[step - 1].astype(F32)
    narrow = channels // cols_n
    for at in range(cols_n):
        @pl.when(col == at)
        def _(at=at):
            r.grad_conv[...] = tap_total[:9, at * narrow : (at + 1) * narrow]

    for g in range(groups - 1):
        place_final(g)
    line_finish(groups - 1)
    place_final(groups - 1)

    for target in range(quarter, 3 * quarter):
        @pl.when(col != target)
        def _(target=target):
            tot(target).wait_send()
    for g in range(groups):
        for kind in KINDS:
            for item in range(half):
                @pl.when(chip != owner_of(kind, item))
                def _(g=g, kind=kind, item=item):
                    along(g, kind, item).wait_send()


def store_kernel(count, *refs):
    copies = [pltpu.make_async_copy(refs[at], refs[count + at], refs[2 * count].at[at]) for at in range(count)]
    for copy in copies:
        copy.start()
    for copy in copies:
        copy.wait()


def on_device(image, conv_taps, w_query, w_key, w_value, w_out, grad_out):
    rows_n, cols_n = lax.axis_size("row"), lax.axis_size("col")
    height, width, channels = image.shape
    tokens = height * width
    own = (height // POOL) * (width // POOL)
    cells_n = cols_n * own
    chips, quarter = cols_n // 2, cols_n // 4
    half = quarter // 2
    shard = 4 * channels // cols_n
    groups = channels // WIDE
    part_lanes = shard // groups
    steps = bits_of(rows_n)
    part_q, part_o = (channels // rows_n, part_lanes), (WIDE // rows_n, shard)
    operands = dict(
        image=image, grad_out=grad_out.reshape(tokens, channels), taps=conv_taps,
        w_query=w_query, w_key=w_key, w_value=w_value, w_out=w_out,
    )
    outputs = dict(
        grad_image=(image.shape, BF16),
        grad_weights=((channels, shard), F32),
        grad_conv=((9, channels // cols_n), F32),
    )
    square = ((channels, channels), BF16)
    flat = ((tokens, channels), BF16)
    edge_cols, edge_rows = ((2, height, channels), BF16), ((2, width, channels), BF16)
    corner = ((4, 8, channels), F32)
    scratch = dict(
        image_v=(image.shape, BF16), grad_out_v=flat, taps_v=(conv_taps.shape, F32),
        w_query_v=square, w_key_v=square, w_value_v=square, w_out_v=square,
        pad1=((height + 2, width, channels), F32), pad2=((height + 2, width, channels), F32),
        stage1=((2, height, channels), F32), stage2=((2, height, channels), F32),
        side1=((2, height + 8, channels), F32), side2=((2, height + 8, channels), F32),
        edge_sum=((2, height, channels), F32), mixed=((height, width, channels), F32),
        windows=((9, own, channels), F32),
        rows_out2=edge_rows,
        hidden=flat, query=flat, dout=flat, grad_query=flat, hidden_in=flat,
        go_split=((2, half, tokens, shard), BF16), go_in=((half, tokens, shard), BF16),
        gq_split=((groups, 2, half, tokens, part_lanes), BF16), gq_in=((groups, half, tokens, part_lanes), BF16),
        att=((groups, tokens, WIDE), BF16), att_in=((groups, tokens, WIDE), BF16),
        pooled=((own, channels), F32), grad_pooled=((own, channels), F32),
        cellbuf=((cols_n, own, channels), BF16),
        keys=((cells_n, channels), BF16), values=((cells_n, channels), BF16),
        key_all=((rows_n, cells_n, channels), BF16), side_all=((rows_n, cells_n, shard), BF16),
        blocks=((cols_n, 2 * own, channels), BF16), blocks_in=((cols_n - 1, 2 * own, channels), BF16),
        tot_all=((cols_n, 2 * own, channels), BF16),
        cols_out1=edge_cols, cols_in1=edge_cols, rows_in1=edge_rows, corners_in1=corner, corners_out1=corner,
        cols_out2=edge_cols, cols_in2=edge_cols, rows_in2=edge_rows, corners_in2=corner, corners_out2=corner,
        terms_q=((groups, half, rows_n) + part_q, BF16), terms_o=((groups, half, rows_n) + part_o, BF16),
        landed_q=((groups, half, rows_n - 1) + part_q, BF16), landed_o=((groups, half, rows_n - 1) + part_o, BF16),
        held_q=((groups, half, rows_n // 2) + part_q, BF16), held_o=((groups, half, rows_n // 2) + part_o, BF16),
        line_q=((groups, chips) + part_q, BF16), line_o=((groups, chips) + part_o, BF16),
        fin_q=((groups, rows_n) + part_q, BF16), fin_o=((groups, rows_n) + part_o, BF16),
        tap_terms=((16, channels), F32),
        tap_out=((16, channels), BF16), tap_in=((rows_n - 1, 16, channels), BF16),
        tap_out2=((16, channels), BF16), tap_in2=((cols_n - 1, 16, channels), BF16),
    )
    sems = dict(
        loaded=(7,),
        halo_send1=(8,), halo_recv1=(8,), halo_send2=(8,), halo_recv2=(8,),
        mate_send=(2 + 2 * groups,), mate_recv=(2 + 2 * groups,),
        cell_send=(cols_n - 1,), cell_recv=(cols_n - 1,),
        block_send=(cols_n - 1,), block_recv=(cols_n - 1,),
        tot_send=(2 * quarter,), tot_recv=(cols_n,),
        half_send=(groups, 2 * half, steps), half_recv=(groups, 2 * half, steps),
        line_send=(groups, 2 * half), line_recv=(groups, chips),
        spread_send=(groups, rows_n - 1), spread_recv=(groups, rows_n - 1),
        tap_send1=(rows_n - 1,), tap_recv1=(rows_n - 1,),
        tap_send2=(cols_n - 1,), tap_recv2=(cols_n - 1,),
        pass_send=(2, rows_n - 1), pass_recv=(2, rows_n - 1),
    )
    names = list(operands) + list(outputs) + list(scratch) + list(sems)
    made = pl.pallas_call(
        partial(block_kernel, rows_n, cols_n, names),
        out_shape=[pltpu.VMEM(*spec) for spec in outputs.values()],
        in_specs=[HBM] * len(operands),
        out_specs=[pl.BlockSpec(memory_space=pltpu.VMEM)] * len(outputs),
        scratch_shapes=[pltpu.VMEM(*spec) for spec in scratch.values()]
        + [pltpu.SemaphoreType.DMA(spec) for spec in sems.values()],
        compiler_params=pltpu.CompilerParams(
            collective_id=0, has_side_effects=True, vmem_limit_bytes=48 * 2**20
        ),
    )(*[pltpu.with_memory_space_constraint(value, pltpu.HBM) for value in operands.values()])
    return tuple(
        pl.pallas_call(
            partial(store_kernel, len(outputs)),
            out_shape=[pltpu.HBM(*spec) for spec in outputs.values()],
            in_specs=[pl.BlockSpec(memory_space=pltpu.VMEM)] * len(outputs),
            out_specs=[HBM] * len(outputs),
            scratch_shapes=[pltpu.SemaphoreType.DMA((len(outputs),))],
        )(*[pltpu.with_memory_space_constraint(value, pltpu.VMEM) for value in made])
    )


def solution(mesh):
    return jax.shard_map(
        on_device,
        mesh=mesh,
        in_specs=(P("row", "col", None), P(), P(), P(), P(), P(), P("row", "col", None)),
        out_specs=(P("row", "col", None), P(None, "col"), P(None, "col")),
        check_vma=False,
    )
```

```python
from functools import partial
from types import SimpleNamespace

import jax
import jax.numpy as jnp
from jax import lax
from jax.experimental import pallas as pl
from jax.experimental.pallas import tpu as pltpu
from jax.sharding import PartitionSpec as P

HD = 64
POOL = 8
LANES = 128
WIDE = 256
EDGE = 16

EPSILON = 1e-05
LOG2E = 1.4426950408889634
MESH = pl.DeviceIdType.MESH
HBM = pl.BlockSpec(memory_space=pltpu.HBM)
DIRECTIONS = ((-1, -1), (-1, 1), (1, -1), (1, 1), (-1, 0), (1, 0), (0, -1), (0, 1))
CORNERS = (0, 1, 2, 3)
ROWS = (4, 5)
COLUMNS = (6, 7)
F32 = jnp.float32
BF16 = jnp.bfloat16


def contract(left, right, at_left, at_right):
    return lax.dot_general(
        left, right, (((at_left,), (at_right,)), ((), ())), preferred_element_type=F32
    )


def split(value):
    high = value.astype(BF16)
    return high, (value - high.astype(F32)).astype(BF16)


def remote(source, target, send, recv, row, col):
    return pltpu.make_async_remote_copy(
        src_ref=source,
        dst_ref=target,
        send_sem=send,
        recv_sem=recv,
        device_id=(row, col),
        device_id_type=MESH,
    )


def bits_of(count):
    return count.bit_length() - 1


def flip(row, bit):
    size = 2**bit
    return row + size * (1 - 2 * lax.rem(row // size, 2))


def block_kernel(rows_n, cols_n, names, *refs):
    r = SimpleNamespace(**dict(zip(names, refs, strict=True)))
    image, grad_out, taps = r.image_v, r.grad_out_v, r.taps_v
    pad1, pad2 = r.pad1, r.pad2
    hidden, query, dout = r.hidden, r.query, r.dout
    grad_query = r.grad_query
    height, width, channels = image.shape
    tokens = height * width
    own = (height // POOL) * (width // POOL)
    per_row = width // POOL
    cells_n = cols_n * own
    shard = 4 * channels // cols_n
    quarter = cols_n // 4
    half = quarter // 2
    groups = channels // WIDE
    part_lanes = shard // groups
    steps = bits_of(rows_n)
    parts = channels // LANES
    row, col = lax.axis_index("row"), lax.axis_index("col")
    chip, core = col // 2, lax.rem(col, 2)
    chips = cols_n // 2
    is_query = chip < half
    is_out = chip >= chips - half
    is_cells = jnp.logical_and(chip >= half, chip < chips - half)

    def row_mate(step):
        return lax.rem(row + step, rows_n)

    def col_mate(step):
        return lax.rem(col + step, cols_n)

    def row_partner(step):
        return (1 - core) * flip(row, step) + core * flip(row, steps - 1 - step)

    def position(of):
        def by(order):
            at = 0
            for step, bit in enumerate(order):
                size = 2**bit
                at = at + lax.rem(row // size + of // size, 2) * 2 ** (steps - 1 - step)
            return at

        return (1 - core) * by(range(steps)) + core * by(range(steps - 1, -1, -1))

    def present(down, right):
        ok = None
        for move, at, count in ((down, row, rows_n), (right, col, cols_n)):
            if move == 0:
                continue
            here = at > 0 if move < 0 else at < count - 1
            ok = here if ok is None else jnp.logical_and(ok, here)
        return ok

    def load(source, target, at):
        return pltpu.make_async_copy(source, target, r.loaded.at[at])

    load_image, load_taps = load(r.image, image, 0), load(r.taps, taps, 1)
    load_grad_out, load_out = load(r.grad_out, grad_out, 2), load(r.w_out, r.w_out_v, 3)
    load_query, load_key = load(r.w_query, r.w_query_v, 4), load(r.w_key, r.w_key_v, 5)
    load_value = load(r.w_value, r.w_value_v, 6)
    load_image.start()
    load_taps.start()

    halo1 = SimpleNamespace(
        pad=pad1, stage=r.stage1, side=r.side1, cols_out=r.cols_out1, cols_in=r.cols_in1, rows_in=r.rows_in1,
        corners_out=r.corners_out1, corners_in=r.corners_in1, send=r.halo_send1, recv=r.halo_recv1,
        edge_rows=(r.image.at[0], r.image.at[height - 1]),
    )
    halo2 = SimpleNamespace(
        pad=pad2, stage=r.stage2, side=r.side2, cols_out=r.cols_out2, cols_in=r.cols_in2, rows_in=r.rows_in2,
        corners_out=r.corners_out2, corners_in=r.corners_in2, send=r.halo_send2, recv=r.halo_recv2,
        edge_rows=(r.rows_out2.at[0], r.rows_out2.at[1]),
    )
    for halo in (halo1, halo2):
        for ref in (halo.cols_in, halo.rows_in, halo.corners_in):
            ref[...] = jnp.zeros_like(ref)

    barrier = pltpu.get_barrier_semaphore()
    greeted = cols_n + rows_n - 2
    for down, right in DIRECTIONS[:4]:
        greeted = greeted + present(down, right).astype(jnp.int32)

        @pl.when(present(down, right))
        def _(down=down, right=right):
            pl.semaphore_signal(barrier, inc=1, device_id=(row + down, col + right), device_id_type=MESH)
    for step in range(1, cols_n):
        pl.semaphore_signal(barrier, inc=1, device_id=(row, col_mate(step)), device_id_type=MESH)
    for step in range(1, rows_n):
        pl.semaphore_signal(barrier, inc=1, device_id=(row_mate(step), col), device_id_type=MESH)

    def edge(halo, at):
        down, right = DIRECTIONS[at]
        edge_row = halo.edge_rows[0 if down < 0 else 1]
        if down == 0:
            source, target = halo.cols_out.at[0 if right < 0 else 1], halo.cols_in.at[1 if right < 0 else 0]
        elif right == 0:
            source, target = edge_row, halo.rows_in.at[1 if down < 0 else 0]
        else:
            source = halo.corners_out.at[(0 if down < 0 else 2) + (0 if right < 0 else 1), pl.ds(0, 1)]
            target = halo.corners_in.at[(2 if down < 0 else 0) + (1 if right < 0 else 0), pl.ds(0, 1)]
        return remote(source, target, halo.send.at[at], halo.recv.at[at], row + down, col + right)

    def pack_edges(halo, first, last):
        for at in range(height):
            for which, value in enumerate((first(at), last(at))):
                halo.stage[which, at : at + 1] = value
                if at == 0 or at == height - 1:
                    halo.corners_out[(0 if at == 0 else 2) + which, 0:1] = value
        halo.cols_out[...] = halo.stage[...].astype(BF16)

    def send_halo(halo, wanted):
        for at in wanted:
            down, right = DIRECTIONS[at]

            @pl.when(present(down, right))
            def _(at=at):
                edge(halo, at).start()

    def wait_halo(halo):
        for at, (down, right) in enumerate(DIRECTIONS):
            @pl.when(present(-down, -right))
            def _(at=at):
                edge(halo, at).wait_recv()

            @pl.when(present(down, right))
            def _(at=at):
                edge(halo, at).wait_send()

    def take_halo(halo):
        halo.pad[0] = halo.rows_in[0].astype(F32)
        halo.pad[height + 1] = halo.rows_in[1].astype(F32)
        for which in range(2):
            halo.side[which, 1 : height + 1] = halo.cols_in[which].astype(F32)
            halo.side[which, 0:1] = halo.corners_in[which, 0:1]
            halo.side[which, height + 1 : height + 2] = halo.corners_in[2 + which, 0:1]

    sublane = lax.broadcasted_iota(jnp.int32, (width, LANES), 0)
    first_column, last_column = sublane == 0, sublane == width - 1

    def from_left(value, halo):
        return jnp.where(first_column, halo, pltpu.roll(value, 1, 0))

    def from_right(value, halo):
        return jnp.where(last_column, halo, pltpu.roll(value, width - 1, 0))

    def lanes_of(part):
        return pl.ds(pl.multiple_of(part * LANES, LANES), LANES)

    pl.semaphore_wait(barrier, greeted)
    send_halo(halo1, ROWS)
    load_image.wait()
    for copy in (load_grad_out, load_out, load_query, load_key, load_value):
        copy.start()
    pack_edges(
        halo1,
        lambda at: image[at, :EDGE].astype(F32)[:1],
        lambda at: image[at, width - EDGE :].astype(F32)[EDGE - 1 :],
    )
    send_halo(halo1, CORNERS + COLUMNS)
    load_taps.wait()
    pad1[0] = jnp.zeros_like(pad1[0])
    pad1[height + 1] = jnp.zeros_like(pad1[0])

    @pl.loop(0, height)
    def _(at):
        pad1[at + 1] = image[at].astype(F32)

    def weights_of(lanes):
        w = [jnp.broadcast_to(taps[i : i + 1, lanes], (width, LANES)) for i in range(9)]
        w[4] = w[4] + 1.0
        return w

    @pl.loop(0, parts)
    def _(part):
        lanes = lanes_of(part)
        w = weights_of(lanes)
        for at in range(height):
            x = [pad1[at + a, :, lanes] for a in range(3)]
            sums = [w[b] * x[0] + w[3 + b] * x[1] + w[6 + b] * x[2] for b in range(3)]
            r.mixed[at, :, lanes] = sums[1] + from_left(sums[0], 0.0) + from_right(sums[2], 0.0)

    chunk = tokens // 2

    def chunk_of(at):
        return pl.ds(pl.multiple_of(at * chunk, chunk), chunk)

    load_grad_out.wait()
    load_out.wait()

    @pl.loop(0, 2)
    def _(at):
        rows = chunk_of(at)
        dout[rows] = contract(grad_out[rows], r.w_out_v[...], 1, 1).astype(BF16)

    for side in range(2):
        for item in range(half):
            at = (2 * item + side) * shard
            r.go_split[side, item] = grad_out[:, at : at + shard]

    def to_mate(source, target, at):
        return remote(source, target, r.mate_send.at[at], r.mate_recv.at[at], row, 2 * chip + 1 - core)

    go_copy = to_mate(r.go_split.at[1 - core], r.go_in, 0)
    go_copy.start()
    wait_halo(halo1)
    take_halo(halo1)

    edge_sublane = lax.broadcasted_iota(jnp.int32, (8, LANES), 0)

    @pl.loop(0, parts)
    def _(part):
        lanes = lanes_of(part)
        w = [jnp.broadcast_to(taps[i : i + 1, lanes], (width, LANES)) for i in range(9)]
        short = [jnp.broadcast_to(taps[i : i + 1, lanes], (height, LANES)) for i in range(9)]
        for which in range(2):
            total = jnp.zeros((height, LANES), F32)
            for a in range(3):
                total = total + short[3 * a + 2 * which] * r.side1[which, a : a + height, lanes]
            r.edge_sum[which, :, lanes] = total
        for cell_row in range(height // POOL):
            pooled = jnp.zeros((width, LANES), F32)
            for at in range(cell_row * POOL, (cell_row + 1) * POOL):
                total = r.mixed[at, :, lanes]
                for edge_at, a in ((0, 0), (height - 1, 2)):
                    if at == edge_at:
                        x = pad1[at + a, :, lanes]
                        total = (
                            total + w[3 * a + 1] * x + from_left(w[3 * a] * x, 0.0) + from_right(w[3 * a + 2] * x, 0.0)
                        )
                left = jnp.where(edge_sublane == 0, r.edge_sum[0, at : at + 1, lanes], 0.0)
                right = jnp.where(edge_sublane == 7, r.edge_sum[1, at : at + 1, lanes], 0.0)
                total = jnp.concatenate(
                    [total[:8] + left, total[8 : width - 8], total[width - 8 :] + right], axis=0
                )
                value = total.astype(BF16)
                hidden[at * width : (at + 1) * width, lanes] = value
                pooled = pooled + value.astype(F32)
            where = slice(cell_row * per_row, (cell_row + 1) * per_row)
            r.pooled[where, lanes] = pooled.reshape(per_row, POOL, LANES).sum(axis=1) / (POOL * POOL)

    pooled = r.pooled[...]
    centre = jnp.mean(pooled, axis=-1, keepdims=True)
    spread = jnp.mean(jnp.square(pooled - centre), axis=-1, keepdims=True)
    inverse = lax.rsqrt(spread + EPSILON)
    standard = (pooled - centre) * inverse
    cellbuf = r.cellbuf
    cellbuf[col] = standard.astype(BF16)

    def cell(step):
        return remote(
            cellbuf.at[col], cellbuf.at[col], r.cell_send.at[step - 1], r.cell_recv.at[step - 1], row, col_mate(step)
        )

    for step in range(1, cols_n):
        cell(step).start()
    hidden_copy = to_mate(hidden, r.hidden_in, 1)
    hidden_copy.start()

    load_query.wait()

    @pl.loop(0, 2)
    def _(at):
        rows = chunk_of(at)
        query[rows] = contract(hidden[rows], r.w_query_v[...], 1, 0).astype(BF16)

    @pl.loop(0, parts)
    def _(part):
        lanes = lanes_of(part)
        for cell_row in range(height // POOL):
            for a in range(3):
                first = cell_row * POOL + a
                total = pad1[first, :, lanes]
                for at in range(first + 1, first + POOL):
                    total = total + pad1[at, :, lanes]
                left, right = (
                    r.side1[which, first : first + POOL, lanes].sum(axis=0, keepdims=True) for which in range(2)
                )
                for b, value in enumerate((from_left(total, left), total, from_right(total, right))):
                    r.windows[3 * a + b, cell_row * per_row : (cell_row + 1) * per_row, lanes] = value.reshape(
                        per_row, POOL, LANES
                    ).sum(axis=1)

    load_key.wait()
    load_value.wait()
    for step in range(1, cols_n):
        cell(step).wait()
    key_cells = jnp.concatenate([cellbuf[at].astype(F32) for at in range(cols_n)], axis=0).astype(BF16)
    r.key_all[row] = key_cells

    def pass_on(ref, at, step):
        return remote(
            ref.at[row], ref.at[row], r.pass_send.at[at, step - 1], r.pass_recv.at[at, step - 1], row_mate(step), col
        )

    @pl.when(is_cells)
    def _():
        for step in range(1, rows_n):
            pass_on(r.key_all, 0, step).start()

    r.keys[...] = contract(key_cells, r.w_key_v[...], 1, 0).astype(BF16)
    r.values[...] = contract(key_cells, r.w_value_v[...], 1, 0).astype(BF16)

    heads = WIDE // HD
    wide_cells = heads * cells_n
    same_head = (
        lax.broadcasted_iota(jnp.int32, (wide_cells, WIDE), 0) // cells_n
        == lax.broadcasted_iota(jnp.int32, (wide_cells, WIDE), 1) // HD
    )
    cell_ones = (
        lax.broadcasted_iota(jnp.int32, (wide_cells, wide_cells), 0) // cells_n
        == lax.broadcasted_iota(jnp.int32, (wide_cells, wide_cells), 1) // cells_n
    ).astype(F32).astype(BF16)
    scale = HD ** (-0.5)
    lane_ones = (
        (
            lax.broadcasted_iota(jnp.int32, (WIDE, wide_cells), 0) // HD
            == lax.broadcasted_iota(jnp.int32, (WIDE, wide_cells), 1) // cells_n
        ).astype(F32) * scale
    ).astype(BF16)
    head_of = lax.broadcasted_iota(jnp.int32, (cells_n, WIDE), 1) // HD
    places = [[(k * shard + g * part_lanes, k) for k in range(quarter)] for g in range(groups)]

    def take(ref, g):
        return jnp.concatenate([ref[:, at : at + part_lanes] for at, _ in places[g]], axis=1)

    def by_head(value):
        total = value[:cells_n]
        for head in range(1, heads):
            total = jnp.where(head_of == head, value[head * cells_n : (head + 1) * cells_n], total)
        return total

    def attend(g):
        def both(ref, factor):
            value = take(ref, g).astype(F32) * factor
            return jnp.where(same_head, jnp.concatenate([value] * heads, axis=0), 0.0).astype(BF16)

        key_wide, value_wide, value_scaled = both(r.keys, 1.0), both(r.values, 1.0), both(r.values, scale)
        queries, douts = take(query, g), take(dout, g)
        expons = jnp.exp2(contract(queries, key_wide, 1, 1) * (scale * LOG2E))
        sums = contract(expons.astype(BF16), cell_ones, 1, 0)
        probabilities = expons / sums
        weights = probabilities.astype(BF16)
        got = contract(weights, value_wide, 1, 0).astype(BF16)
        r.att[g] = got
        grad_probs = contract(douts, value_scaled, 1, 1)
        deltas = contract((douts.astype(F32) * got.astype(F32)).astype(BF16), lane_ones, 1, 0)
        grad_scores = (probabilities * (grad_probs - deltas)).astype(BF16)
        grad_queries = contract(grad_scores, key_wide, 1, 0).astype(BF16)
        for at, k in places[g]:
            piece = grad_queries[:, k * part_lanes : (k + 1) * part_lanes]
            grad_query[:, at : at + part_lanes] = piece
            r.gq_split[g, k % 2, k // 2] = piece
        to_mate(r.gq_split.at[g, 1 - core], r.gq_in.at[g], 2 + g).start()
        to_mate(r.att.at[g], r.att_in.at[g], 2 + groups + g).start()
        grad_key = by_head(contract(grad_scores, queries, 0, 0))
        grad_value = by_head(contract(weights, douts, 0, 0))
        for owner in range(cols_n):
            rows = slice(owner * own, (owner + 1) * own)
            both_rows = jnp.concatenate([grad_key[rows], grad_value[rows]], axis=0).astype(BF16)
            for at, k in places[g]:
                r.blocks[owner, :, at : at + part_lanes] = both_rows[:, k * part_lanes : (k + 1) * part_lanes]

    def block(step):
        owner = col_mate(step)
        return remote(
            r.blocks.at[owner], r.blocks_in.at[step - 1], r.block_send.at[step - 1], r.block_recv.at[step - 1], row, owner
        )

    KINDS = (0, 1)
    made = (r.terms_q, r.terms_o)
    landed = (r.landed_q, r.landed_o)
    held = (r.held_q, r.held_o)
    line = (r.line_q, r.line_o)
    fin = (r.fin_q, r.fin_o)

    def terms(g):
        to_mate(r.gq_split.at[g, 1 - core], r.gq_in.at[g], 2 + g).wait()
        to_mate(r.att.at[g], r.att_in.at[g], 2 + groups + g).wait()
        for item in range(half):
            for_query = contract(hidden[...], r.gq_split[g, core, item], 0, 0) + contract(
                r.hidden_in[...], r.gq_in[g, item], 0, 0
            )
            for_out = contract(r.att[g], r.go_split[core, item], 0, 0) + contract(
                r.att_in[g], r.go_in[item], 0, 0
            )
            for kind, value in enumerate((for_query, for_out)):
                value = value.astype(BF16)
                size = value.shape[0] // rows_n
                for at in range(rows_n):
                    made[kind][g, item, position(at)] = value[at * size : (at + 1) * size]

    def halving(g, kind, item, step):
        count = rows_n >> (step + 1)
        base = made[kind] if step == 0 else held[kind]
        offset = rows_n - 2 * count
        number = kind * half + item
        return remote(
            base.at[g, item, pl.ds(count, count)], landed[kind].at[g, item, pl.ds(offset, count)],
            r.half_send.at[g, number, step], r.half_recv.at[g, number, step], row_partner(step), col,
        )

    def halve_start(g, step):
        for kind in KINDS:
            for item in range(half):
                halving(g, kind, item, step).start()

    def halve_finish(g, step):
        count = rows_n >> (step + 1)
        offset = rows_n - 2 * count
        for kind in KINDS:
            for item in range(half):
                halving(g, kind, item, step).wait()
                base = made[kind] if step == 0 else held[kind]
                held[kind][g, item, 0:count] = (
                    base[g, item, 0:count].astype(F32)
                    + landed[kind][g, item, offset : offset + count].astype(F32)
                ).astype(BF16)
                if step < steps - 1:
                    halving(g, kind, item, step + 1).start()
                else:
                    @pl.when(chip != owner_of(kind, item))
                    def _(kind=kind, item=item):
                        along(g, kind, item).start()

    def owner_of(kind, item):
        return item if kind == 0 else chips - half + item

    def along(g, kind, item):
        number = kind * half + item
        return remote(
            held[kind].at[g, item, 0], line[kind].at[g, chip],
            r.line_send.at[g, number], r.line_recv.at[g, chip], row, 2 * owner_of(kind, item) + core,
        )

    def arrived(g, kind, source):
        return remote(
            held[kind].at[g, 0, 0], line[kind].at[g, source],
            r.line_send.at[g, 0], r.line_recv.at[g, source], row, 2 * source + core,
        )

    def spread_out(g, kind, step):
        return remote(
            fin[kind].at[g, row], fin[kind].at[g, row],
            r.spread_send.at[g, step - 1], r.spread_recv.at[g, step - 1], row_mate(step), col,
        )

    def each_owner(body):
        for kind, here, item in ((0, is_query, chip), (1, is_out, chip - (chips - half))):
            @pl.when(here)
            def _(kind=kind, item=item):
                body(kind, item)

    def line_finish(g):
        def body(kind, item):
            total = held[kind][g, item, 0].astype(F32)
            for step in range(1, chips):
                source = lax.rem(chip + step, chips)
                arrived(g, kind, source).wait_recv()
                total = total + line[kind][g, source].astype(F32)
            fin[kind][g, row] = total.astype(BF16)
            for step in range(1, rows_n):
                spread_out(g, kind, step).start()

        each_owner(body)

    def place_final(g):
        def body(kind, item):
            for step in range(1, rows_n):
                spread_out(g, kind, step).wait()
            for part in range(rows_n):
                value = fin[kind][g, part].astype(F32)
                if kind == 0:
                    size = channels // rows_n
                    r.grad_weights[part * size : (part + 1) * size, g * part_lanes : (g + 1) * part_lanes] = value
                else:
                    size = WIDE // rows_n
                    k = (part * size) // part_lanes
                    at = k * shard + g * part_lanes + part * size - k * part_lanes
                    r.grad_weights[at : at + size] = value

        each_owner(body)

    go_copy.wait()
    hidden_copy.wait()
    for g in range(groups):
        attend(g)
    for step in range(1, cols_n):
        block(step).start()
    for g in range(groups):
        terms(g)
        halve_start(g, 0)

    @pl.loop(0, 2)
    def _(at):
        rows = chunk_of(at)
        value = contract(grad_query[rows], r.w_query_v[...], 1, 1) + grad_out[rows].astype(F32)
        pad2[pl.ds(1 + at * (height // 2), height // 2)] = value.reshape(height // 2, width, channels)

    halve_finish(0, 0)

    for at in range(height):
        for which, value in enumerate((pad2[at + 1, 0:1], pad2[at + 1, width - 1 : width])):
            r.stage1[which, at : at + 1] = value
    r.tap_terms[...] = jnp.zeros_like(r.tap_terms)

    @pl.loop(0, parts)
    def _(part):
        lanes = lanes_of(part)
        sums = [jnp.zeros((8, LANES), F32) for _ in range(9)]
        for at in range(height):
            value = pad2[at + 1, :, lanes]
            shifted = [from_right(value, 0.0), value, from_left(value, 0.0)]
            for a in range(3):
                x = pad1[at + a, :, lanes]
                for b in range(3):
                    sums[3 * a + b] = sums[3 * a + b] + (shifted[b] * x).reshape(width // 8, 8, LANES).sum(axis=0)
        for i in range(9):
            total = sums[i].sum(axis=0, keepdims=True)
            if i % 3 != 1:
                which = 0 if i % 3 == 0 else 1
                product = r.stage1[which, :, lanes] * r.side1[which, i // 3 : i // 3 + height, lanes]
                total = total + product.sum(axis=0, keepdims=True)
            r.tap_terms[i : i + 1, lanes] = total

    totals = r.blocks[col].astype(F32)
    for step in range(1, cols_n):
        block(step).wait()
        totals = totals + r.blocks_in[step - 1].astype(F32)
    high, low = split(totals)
    tot_all = r.tot_all
    tot_all[col] = high

    def tot(target):
        return remote(
            tot_all.at[col], tot_all.at[col], r.tot_send.at[target - quarter], r.tot_recv.at[col], row, target
        )

    def tot_from(source):
        return remote(
            tot_all.at[source], tot_all.at[source], r.tot_send.at[0], r.tot_recv.at[source], row, source
        )

    for target in range(quarter, 3 * quarter):
        @pl.when(col != target)
        def _(target=target):
            tot(target).start()

    both_parts = jnp.concatenate([high, low], axis=0)
    by_key = contract(both_parts, r.w_key_v[...], 1, 1)
    by_value = contract(both_parts, r.w_value_v[...], 1, 1)
    grad_normed = by_key[:own] + by_key[2 * own : 3 * own] + by_value[own : 2 * own] + by_value[3 * own :]
    grad_pooled = (
        grad_normed
        - jnp.mean(grad_normed, axis=-1, keepdims=True)
        - standard * jnp.mean(grad_normed * standard, axis=-1, keepdims=True)
    ) * (inverse / (POOL * POOL))
    r.grad_pooled[...] = grad_pooled
    narrow = channels // cols_n
    for i in range(9):
        r.tap_terms[i : i + 1] = r.tap_terms[i : i + 1] + (r.windows[i] * grad_pooled).sum(axis=0, keepdims=True)
    for at in range(cols_n):
        r.tap_out[at] = r.tap_terms[:, at * narrow : (at + 1) * narrow].astype(BF16)

    def tap_first(step):
        return remote(
            r.tap_out.at[col_mate(step)], r.tap_in.at[step - 1],
            r.tap_send1.at[step - 1], r.tap_recv1.at[step - 1], row, col_mate(step),
        )

    def tap_second(step):
        return remote(
            r.tap_out2, r.tap_in2.at[step - 1], r.tap_send2.at[step - 1], r.tap_recv2.at[step - 1], row_mate(step), col
        )

    for step in range(1, cols_n):
        tap_first(step).start()

    halve_finish(1, 0)

    @pl.loop(0, parts)
    def _(part):
        lanes = lanes_of(part)
        for cell_row in range(height // POOL):
            over = jnp.concatenate(
                [
                    jnp.broadcast_to(r.grad_pooled[at : at + 1, lanes], (POOL, LANES))
                    for at in range(cell_row * per_row, (cell_row + 1) * per_row)
                ],
                axis=0,
            )
            for at in range(cell_row * POOL, (cell_row + 1) * POOL):
                value = pad2[at + 1, :, lanes] + over
                pad2[at + 1, :, lanes] = value
                if at == 0 or at == height - 1:
                    r.rows_out2[0 if at == 0 else 1, :, lanes] = value.astype(BF16)

    pack_edges(halo2, lambda at: pad2[at + 1, 0:1], lambda at: pad2[at + 1, width - 1 : width])
    send_halo(halo2, range(8))

    for step in range(1, steps):
        halve_finish(0, step)
    for g in range(2, groups):
        halve_finish(g, 0)
    for g in range(1, groups - 1):
        for step in range(1, steps):
            halve_finish(g, step)

    @pl.when(is_cells)
    def _():
        for step in range(1, cols_n):
            tot_from(col_mate(step)).wait_recv()
        is_key = col < 2 * quarter
        sides = []
        for at in range(cols_n):
            value = tot_all[at].astype(F32)
            sides.append(jnp.where(is_key, value[:own], value[own:]))
        value = jnp.concatenate(sides, axis=0)
        mine = value[:, :shard]
        for k in range(1, quarter):
            mine = jnp.where(lax.rem(col, quarter) == k, value[:, k * shard : (k + 1) * shard], mine)
        r.side_all[row] = mine.astype(BF16)
        for step in range(1, rows_n):
            pass_on(r.side_all, 1, step).start()

    tap_total = r.tap_out[col].astype(F32)
    for step in range(1, cols_n):
        tap_first(step).wait()
        tap_total = tap_total + r.tap_in[step - 1].astype(F32)
    r.tap_out2[...] = tap_total.astype(BF16)
    for step in range(1, rows_n):
        tap_second(step).start()

    for step in range(1, steps):
        halve_finish(groups - 1, step)
    line_finish(0)
    wait_halo(halo2)
    take_halo(halo2)

    @pl.loop(0, parts)
    def _(part):
        lanes = lanes_of(part)
        w = weights_of(lanes)
        short = [jnp.broadcast_to(taps[i : i + 1, lanes], (height, LANES)) for i in range(9)]
        for which in range(2):
            total = jnp.zeros((height, LANES), F32)
            for a in range(3):
                total = total + short[3 * a + 2 - 2 * which] * r.side2[which, 2 - a : 2 - a + height, lanes]
            r.edge_sum[which, :, lanes] = total
        for at in range(height):
            x = [pad2[at + 2 - a, :, lanes] for a in range(3)]
            sums = [w[b] * x[0] + w[3 + b] * x[1] + w[6 + b] * x[2] for b in range(3)]
            total = (
                sums[1]
                + from_right(sums[0], r.edge_sum[1, at : at + 1, lanes])
                + from_left(sums[2], r.edge_sum[0, at : at + 1, lanes])
            )
            r.grad_image[at, :, lanes] = total.astype(BF16)

    for g in range(1, groups - 1):
        line_finish(g)

    @pl.when(is_cells)
    def _():
        for at, ref in enumerate((r.key_all, r.side_all)):
            for step in range(1, rows_n):
                pass_on(ref, at, step).wait()
        keys = r.key_all[...].reshape(rows_n * cells_n, channels)
        sides = r.side_all[...].reshape(rows_n * cells_n, shard)
        r.grad_weights[...] = contract(keys, sides, 0, 0)

    tap_total = r.tap_out2[...].astype(F32)
    for step in range(1, rows_n):
        tap_second(step).wait()
        tap_total = tap_total + r.tap_in2[step - 1].astype(F32)
    r.grad_conv[...] = tap_total[:9]

    line_finish(groups - 1)
    for g in range(groups):
        place_final(g)

    for target in range(quarter, 3 * quarter):
        @pl.when(col != target)
        def _(target=target):
            tot(target).wait_send()
    for g in range(groups):
        for kind in KINDS:
            for item in range(half):
                @pl.when(chip != owner_of(kind, item))
                def _(g=g, kind=kind, item=item):
                    along(g, kind, item).wait_send()


def store_kernel(count, *refs):
    copies = [pltpu.make_async_copy(refs[at], refs[count + at], refs[2 * count].at[at]) for at in range(count)]
    for copy in copies:
        copy.start()
    for copy in copies:
        copy.wait()


def on_device(image, conv_taps, w_query, w_key, w_value, w_out, grad_out):
    rows_n, cols_n = lax.axis_size("row"), lax.axis_size("col")
    height, width, channels = image.shape
    tokens = height * width
    own = (height // POOL) * (width // POOL)
    cells_n = cols_n * own
    chips, quarter = cols_n // 2, cols_n // 4
    half = quarter // 2
    shard = 4 * channels // cols_n
    groups = channels // WIDE
    part_lanes = shard // groups
    steps = bits_of(rows_n)
    part_q, part_o = (channels // rows_n, part_lanes), (WIDE // rows_n, shard)
    operands = dict(
        image=image, grad_out=grad_out.reshape(tokens, channels), taps=conv_taps,
        w_query=w_query, w_key=w_key, w_value=w_value, w_out=w_out,
    )
    outputs = dict(
        grad_image=(image.shape, BF16),
        grad_weights=((channels, shard), F32),
        grad_conv=((9, channels // cols_n), F32),
    )
    square = ((channels, channels), BF16)
    flat = ((tokens, channels), BF16)
    edge_cols, edge_rows = ((2, height, channels), BF16), ((2, width, channels), BF16)
    corner = ((4, 8, channels), F32)
    scratch = dict(
        image_v=(image.shape, BF16), grad_out_v=flat, taps_v=(conv_taps.shape, F32),
        w_query_v=square, w_key_v=square, w_value_v=square, w_out_v=square,
        pad1=((height + 2, width, channels), F32), pad2=((height + 2, width, channels), F32),
        stage1=((2, height, channels), F32), stage2=((2, height, channels), F32),
        side1=((2, height + 8, channels), F32), side2=((2, height + 8, channels), F32),
        edge_sum=((2, height, channels), F32), mixed=((height, width, channels), F32),
        windows=((9, own, channels), F32),
        rows_out2=edge_rows,
        hidden=flat, query=flat, dout=flat, grad_query=flat, hidden_in=flat,
        go_split=((2, half, tokens, shard), BF16), go_in=((half, tokens, shard), BF16),
        gq_split=((groups, 2, half, tokens, part_lanes), BF16), gq_in=((groups, half, tokens, part_lanes), BF16),
        att=((groups, tokens, WIDE), BF16), att_in=((groups, tokens, WIDE), BF16),
        pooled=((own, channels), F32), grad_pooled=((own, channels), F32),
        cellbuf=((cols_n, own, channels), BF16),
        keys=((cells_n, channels), BF16), values=((cells_n, channels), BF16),
        key_all=((rows_n, cells_n, channels), BF16), side_all=((rows_n, cells_n, shard), BF16),
        blocks=((cols_n, 2 * own, channels), BF16), blocks_in=((cols_n - 1, 2 * own, channels), BF16),
        tot_all=((cols_n, 2 * own, channels), BF16),
        cols_out1=edge_cols, cols_in1=edge_cols, rows_in1=edge_rows, corners_in1=corner, corners_out1=corner,
        cols_out2=edge_cols, cols_in2=edge_cols, rows_in2=edge_rows, corners_in2=corner, corners_out2=corner,
        terms_q=((groups, half, rows_n) + part_q, BF16), terms_o=((groups, half, rows_n) + part_o, BF16),
        landed_q=((groups, half, rows_n - 1) + part_q, BF16), landed_o=((groups, half, rows_n - 1) + part_o, BF16),
        held_q=((groups, half, rows_n // 2) + part_q, BF16), held_o=((groups, half, rows_n // 2) + part_o, BF16),
        line_q=((groups, chips) + part_q, BF16), line_o=((groups, chips) + part_o, BF16),
        fin_q=((groups, rows_n) + part_q, BF16), fin_o=((groups, rows_n) + part_o, BF16),
        tap_terms=((16, channels), F32),
        tap_out=((cols_n, 16, channels // cols_n), BF16), tap_in=((cols_n - 1, 16, channels // cols_n), BF16),
        tap_out2=((16, channels // cols_n), BF16), tap_in2=((rows_n - 1, 16, channels // cols_n), BF16),
    )
    sems = dict(
        loaded=(7,),
        halo_send1=(8,), halo_recv1=(8,), halo_send2=(8,), halo_recv2=(8,),
        mate_send=(2 + 2 * groups,), mate_recv=(2 + 2 * groups,),
        cell_send=(cols_n - 1,), cell_recv=(cols_n - 1,),
        block_send=(cols_n - 1,), block_recv=(cols_n - 1,),
        tot_send=(2 * quarter,), tot_recv=(cols_n,),
        half_send=(groups, 2 * half, steps), half_recv=(groups, 2 * half, steps),
        line_send=(groups, 2 * half), line_recv=(groups, chips),
        spread_send=(groups, rows_n - 1), spread_recv=(groups, rows_n - 1),
        tap_send1=(cols_n - 1,), tap_recv1=(cols_n - 1,),
        tap_send2=(rows_n - 1,), tap_recv2=(rows_n - 1,),
        pass_send=(2, rows_n - 1), pass_recv=(2, rows_n - 1),
    )
    names = list(operands) + list(outputs) + list(scratch) + list(sems)
    made = pl.pallas_call(
        partial(block_kernel, rows_n, cols_n, names),
        out_shape=[pltpu.VMEM(*spec) for spec in outputs.values()],
        in_specs=[HBM] * len(operands),
        out_specs=[pl.BlockSpec(memory_space=pltpu.VMEM)] * len(outputs),
        scratch_shapes=[pltpu.VMEM(*spec) for spec in scratch.values()]
        + [pltpu.SemaphoreType.DMA(spec) for spec in sems.values()],
        compiler_params=pltpu.CompilerParams(
            collective_id=0, has_side_effects=True, vmem_limit_bytes=48 * 2**20
        ),
    )(*[pltpu.with_memory_space_constraint(value, pltpu.HBM) for value in operands.values()])
    return tuple(
        pl.pallas_call(
            partial(store_kernel, len(outputs)),
            out_shape=[pltpu.HBM(*spec) for spec in outputs.values()],
            in_specs=[pl.BlockSpec(memory_space=pltpu.VMEM)] * len(outputs),
            out_specs=[HBM] * len(outputs),
            scratch_shapes=[pltpu.SemaphoreType.DMA((len(outputs),))],
        )(*[pltpu.with_memory_space_constraint(value, pltpu.VMEM) for value in made])
    )


def solution(mesh):
    return jax.shard_map(
        on_device,
        mesh=mesh,
        in_specs=(P("row", "col", None), P(), P(), P(), P(), P(), P("row", "col", None)),
        out_specs=(P("row", "col", None), P(None, "col"), P(None, "col")),
        check_vma=False,
    )
```

```python
from functools import partial
from types import SimpleNamespace

import jax
import jax.numpy as jnp
from jax import lax
from jax.experimental import pallas as pl
from jax.experimental.pallas import tpu as pltpu
from jax.sharding import PartitionSpec as P

HD = 64
POOL = 8
LANES = 128
WIDE = 256
EDGE = 16

EPSILON = 1e-05
LOG2E = 1.4426950408889634
MESH = pl.DeviceIdType.MESH
HBM = pl.BlockSpec(memory_space=pltpu.HBM)
DIRECTIONS = ((-1, -1), (-1, 1), (1, -1), (1, 1), (-1, 0), (1, 0), (0, -1), (0, 1))
CORNERS = (0, 1, 2, 3)
ROWS = (4, 5)
COLUMNS = (6, 7)
F32 = jnp.float32
BF16 = jnp.bfloat16


def contract(left, right, at_left, at_right):
    return lax.dot_general(
        left, right, (((at_left,), (at_right,)), ((), ())), preferred_element_type=F32
    )


def split(value):
    high = value.astype(BF16)
    return high, (value - high.astype(F32)).astype(BF16)


def remote(source, target, send, recv, row, col):
    return pltpu.make_async_remote_copy(
        src_ref=source,
        dst_ref=target,
        send_sem=send,
        recv_sem=recv,
        device_id=(row, col),
        device_id_type=MESH,
    )


def bits_of(count):
    return count.bit_length() - 1


def flip(row, bit):
    size = 2**bit
    return row + size * (1 - 2 * lax.rem(row // size, 2))


def block_kernel(rows_n, cols_n, names, *refs):
    r = SimpleNamespace(**dict(zip(names, refs, strict=True)))
    image, grad_out, taps = r.image_v, r.grad_out_v, r.taps_v
    pad1, pad2 = r.pad1, r.pad2
    hidden, query, dout = r.hidden, r.query, r.dout
    grad_query = r.grad_query
    height, width, channels = image.shape
    tokens = height * width
    own = (height // POOL) * (width // POOL)
    per_row = width // POOL
    cells_n = cols_n * own
    shard = 4 * channels // cols_n
    quarter = cols_n // 4
    half = quarter // 2
    groups = channels // WIDE
    part_lanes = shard // groups
    steps = bits_of(rows_n)
    parts = channels // LANES
    row, col = lax.axis_index("row"), lax.axis_index("col")
    chip, core = col // 2, lax.rem(col, 2)
    chips = cols_n // 2
    is_query = chip < half
    is_out = chip >= chips - half
    is_cells = jnp.logical_and(chip >= half, chip < chips - half)

    def row_mate(step):
        return lax.rem(row + step, rows_n)

    def col_mate(step):
        return lax.rem(col + step, cols_n)

    def row_partner(step):
        return (1 - core) * flip(row, step) + core * flip(row, steps - 1 - step)

    def position(of):
        def by(order):
            at = 0
            for step, bit in enumerate(order):
                size = 2**bit
                at = at + lax.rem(row // size + of // size, 2) * 2 ** (steps - 1 - step)
            return at

        return (1 - core) * by(range(steps)) + core * by(range(steps - 1, -1, -1))

    def present(down, right):
        ok = None
        for move, at, count in ((down, row, rows_n), (right, col, cols_n)):
            if move == 0:
                continue
            here = at > 0 if move < 0 else at < count - 1
            ok = here if ok is None else jnp.logical_and(ok, here)
        return ok

    def load(source, target, at):
        return pltpu.make_async_copy(source, target, r.loaded.at[at])

    load_image, load_taps = load(r.image, image, 0), load(r.taps, taps, 1)
    load_grad_out, load_out = load(r.grad_out, grad_out, 2), load(r.w_out, r.w_out_v, 3)
    load_query, load_key = load(r.w_query, r.w_query_v, 4), load(r.w_key, r.w_key_v, 5)
    load_value = load(r.w_value, r.w_value_v, 6)
    load_image.start()
    load_taps.start()

    halo1 = SimpleNamespace(
        pad=pad1, stage=r.stage1, side=r.side1, cols_out=r.cols_out1, cols_in=r.cols_in1, rows_in=r.rows_in1,
        corners_out=r.corners_out1, corners_in=r.corners_in1, send=r.halo_send1, recv=r.halo_recv1,
        edge_rows=(r.image.at[0], r.image.at[height - 1]),
    )
    halo2 = SimpleNamespace(
        pad=pad2, stage=r.stage2, side=r.side2, cols_out=r.cols_out2, cols_in=r.cols_in2, rows_in=r.rows_in2,
        corners_out=r.corners_out2, corners_in=r.corners_in2, send=r.halo_send2, recv=r.halo_recv2,
        edge_rows=(r.rows_out2.at[0], r.rows_out2.at[1]),
    )
    for halo in (halo1, halo2):
        for ref in (halo.cols_in, halo.rows_in, halo.corners_in):
            ref[...] = jnp.zeros_like(ref)

    barrier = pltpu.get_barrier_semaphore()
    greeted = cols_n + rows_n - 2
    for down, right in DIRECTIONS[:4]:
        greeted = greeted + present(down, right).astype(jnp.int32)

        @pl.when(present(down, right))
        def _(down=down, right=right):
            pl.semaphore_signal(barrier, inc=1, device_id=(row + down, col + right), device_id_type=MESH)
    for step in range(1, cols_n):
        pl.semaphore_signal(barrier, inc=1, device_id=(row, col_mate(step)), device_id_type=MESH)
    for step in range(1, rows_n):
        pl.semaphore_signal(barrier, inc=1, device_id=(row_mate(step), col), device_id_type=MESH)

    def edge(halo, at):
        down, right = DIRECTIONS[at]
        edge_row = halo.edge_rows[0 if down < 0 else 1]
        if down == 0:
            source, target = halo.cols_out.at[0 if right < 0 else 1], halo.cols_in.at[1 if right < 0 else 0]
        elif right == 0:
            source, target = edge_row, halo.rows_in.at[1 if down < 0 else 0]
        else:
            source = halo.corners_out.at[(0 if down < 0 else 2) + (0 if right < 0 else 1), pl.ds(0, 1)]
            target = halo.corners_in.at[(2 if down < 0 else 0) + (1 if right < 0 else 0), pl.ds(0, 1)]
        return remote(source, target, halo.send.at[at], halo.recv.at[at], row + down, col + right)

    def pack_edges(halo, first, last):
        for at in range(height):
            for which, value in enumerate((first(at), last(at))):
                halo.stage[which, at : at + 1] = value
                if at == 0 or at == height - 1:
                    halo.corners_out[(0 if at == 0 else 2) + which, 0:1] = value
        halo.cols_out[...] = halo.stage[...].astype(BF16)

    def send_halo(halo, wanted):
        for at in wanted:
            down, right = DIRECTIONS[at]

            @pl.when(present(down, right))
            def _(at=at):
                edge(halo, at).start()

    def wait_halo(halo):
        for at, (down, right) in enumerate(DIRECTIONS):
            @pl.when(present(-down, -right))
            def _(at=at):
                edge(halo, at).wait_recv()

            @pl.when(present(down, right))
            def _(at=at):
                edge(halo, at).wait_send()

    def take_halo(halo):
        halo.pad[0] = halo.rows_in[0].astype(F32)
        halo.pad[height + 1] = halo.rows_in[1].astype(F32)
        for which in range(2):
            halo.side[which, 1 : height + 1] = halo.cols_in[which].astype(F32)
            halo.side[which, 0:1] = halo.corners_in[which, 0:1]
            halo.side[which, height + 1 : height + 2] = halo.corners_in[2 + which, 0:1]

    sublane = lax.broadcasted_iota(jnp.int32, (width, LANES), 0)
    first_column, last_column = sublane == 0, sublane == width - 1

    def from_left(value, halo):
        return jnp.where(first_column, halo, pltpu.roll(value, 1, 0))

    def from_right(value, halo):
        return jnp.where(last_column, halo, pltpu.roll(value, width - 1, 0))

    def lanes_of(part):
        return pl.ds(pl.multiple_of(part * LANES, LANES), LANES)

    pl.semaphore_wait(barrier, greeted)
    send_halo(halo1, ROWS)
    load_image.wait()
    for copy in (load_grad_out, load_out, load_query, load_key, load_value):
        copy.start()
    pack_edges(
        halo1,
        lambda at: image[at, :EDGE].astype(F32)[:1],
        lambda at: image[at, width - EDGE :].astype(F32)[EDGE - 1 :],
    )
    send_halo(halo1, CORNERS + COLUMNS)
    load_taps.wait()
    pad1[0] = jnp.zeros_like(pad1[0])
    pad1[height + 1] = jnp.zeros_like(pad1[0])

    @pl.loop(0, height)
    def _(at):
        pad1[at + 1] = image[at].astype(F32)

    def weights_of(lanes):
        w = [jnp.broadcast_to(taps[i : i + 1, lanes], (width, LANES)) for i in range(9)]
        w[4] = w[4] + 1.0
        return w

    @pl.loop(0, parts)
    def _(part):
        lanes = lanes_of(part)
        w = weights_of(lanes)
        for at in range(height):
            x = [pad1[at + a, :, lanes] for a in range(3)]
            sums = [w[b] * x[0] + w[3 + b] * x[1] + w[6 + b] * x[2] for b in range(3)]
            r.mixed[at, :, lanes] = sums[1] + from_left(sums[0], 0.0) + from_right(sums[2], 0.0)

    chunk = tokens // 2

    def chunk_of(at):
        return pl.ds(pl.multiple_of(at * chunk, chunk), chunk)

    load_grad_out.wait()
    load_out.wait()

    @pl.loop(0, 2)
    def _(at):
        rows = chunk_of(at)
        dout[rows] = contract(grad_out[rows], r.w_out_v[...], 1, 1).astype(BF16)

    for side in range(2):
        for item in range(half):
            at = (2 * item + side) * shard
            r.go_split[side, item] = grad_out[:, at : at + shard]

    def to_mate(source, target, at):
        return remote(source, target, r.mate_send.at[at], r.mate_recv.at[at], row, 2 * chip + 1 - core)

    go_copy = to_mate(r.go_split.at[1 - core], r.go_in, 0)
    go_copy.start()
    wait_halo(halo1)
    take_halo(halo1)

    edge_sublane = lax.broadcasted_iota(jnp.int32, (8, LANES), 0)

    @pl.loop(0, parts)
    def _(part):
        lanes = lanes_of(part)
        w = [jnp.broadcast_to(taps[i : i + 1, lanes], (width, LANES)) for i in range(9)]
        short = [jnp.broadcast_to(taps[i : i + 1, lanes], (height, LANES)) for i in range(9)]
        for which in range(2):
            total = jnp.zeros((height, LANES), F32)
            for a in range(3):
                total = total + short[3 * a + 2 * which] * r.side1[which, a : a + height, lanes]
            r.edge_sum[which, :, lanes] = total
        for cell_row in range(height // POOL):
            pooled = jnp.zeros((width, LANES), F32)
            for at in range(cell_row * POOL, (cell_row + 1) * POOL):
                total = r.mixed[at, :, lanes]
                for edge_at, a in ((0, 0), (height - 1, 2)):
                    if at == edge_at:
                        x = pad1[at + a, :, lanes]
                        total = (
                            total + w[3 * a + 1] * x + from_left(w[3 * a] * x, 0.0) + from_right(w[3 * a + 2] * x, 0.0)
                        )
                left = jnp.where(edge_sublane == 0, r.edge_sum[0, at : at + 1, lanes], 0.0)
                right = jnp.where(edge_sublane == 7, r.edge_sum[1, at : at + 1, lanes], 0.0)
                total = jnp.concatenate(
                    [total[:8] + left, total[8 : width - 8], total[width - 8 :] + right], axis=0
                )
                value = total.astype(BF16)
                hidden[at * width : (at + 1) * width, lanes] = value
                pooled = pooled + value.astype(F32)
            where = slice(cell_row * per_row, (cell_row + 1) * per_row)
            r.pooled[where, lanes] = pooled.reshape(per_row, POOL, LANES).sum(axis=1) / (POOL * POOL)

    pooled = r.pooled[...]
    centre = jnp.mean(pooled, axis=-1, keepdims=True)
    spread = jnp.mean(jnp.square(pooled - centre), axis=-1, keepdims=True)
    inverse = lax.rsqrt(spread + EPSILON)
    standard = (pooled - centre) * inverse
    cellbuf = r.cellbuf
    cellbuf[col] = standard.astype(BF16)

    def cell(step):
        return remote(
            cellbuf.at[col], cellbuf.at[col], r.cell_send.at[step - 1], r.cell_recv.at[step - 1], row, col_mate(step)
        )

    for step in range(1, cols_n):
        cell(step).start()
    hidden_copy = to_mate(hidden, r.hidden_in, 1)
    hidden_copy.start()

    load_query.wait()

    @pl.loop(0, 2)
    def _(at):
        rows = chunk_of(at)
        query[rows] = contract(hidden[rows], r.w_query_v[...], 1, 0).astype(BF16)

    @pl.loop(0, parts)
    def _(part):
        lanes = lanes_of(part)
        for cell_row in range(height // POOL):
            for a in range(3):
                first = cell_row * POOL + a
                total = pad1[first, :, lanes]
                for at in range(first + 1, first + POOL):
                    total = total + pad1[at, :, lanes]
                left, right = (
                    r.side1[which, first : first + POOL, lanes].sum(axis=0, keepdims=True) for which in range(2)
                )
                for b, value in enumerate((from_left(total, left), total, from_right(total, right))):
                    r.windows[3 * a + b, cell_row * per_row : (cell_row + 1) * per_row, lanes] = value.reshape(
                        per_row, POOL, LANES
                    ).sum(axis=1)

    load_key.wait()
    load_value.wait()
    for step in range(1, cols_n):
        cell(step).wait()
    key_cells = jnp.concatenate([cellbuf[at].astype(F32) for at in range(cols_n)], axis=0).astype(BF16)
    r.key_all[row] = key_cells

    def pass_on(ref, at, step):
        return remote(
            ref.at[row], ref.at[row], r.pass_send.at[at, step - 1], r.pass_recv.at[at, step - 1], row_mate(step), col
        )

    @pl.when(is_cells)
    def _():
        for step in range(1, rows_n):
            pass_on(r.key_all, 0, step).start()

    r.keys[...] = contract(key_cells, r.w_key_v[...], 1, 0).astype(BF16)
    r.values[...] = contract(key_cells, r.w_value_v[...], 1, 0).astype(BF16)

    heads = WIDE // HD
    wide_cells = heads * cells_n
    same_head = (
        lax.broadcasted_iota(jnp.int32, (wide_cells, WIDE), 0) // cells_n
        == lax.broadcasted_iota(jnp.int32, (wide_cells, WIDE), 1) // HD
    )
    cell_ones = (
        lax.broadcasted_iota(jnp.int32, (wide_cells, wide_cells), 0) // cells_n
        == lax.broadcasted_iota(jnp.int32, (wide_cells, wide_cells), 1) // cells_n
    ).astype(F32).astype(BF16)
    scale = HD ** (-0.5)
    lane_ones = (
        (
            lax.broadcasted_iota(jnp.int32, (WIDE, wide_cells), 0) // HD
            == lax.broadcasted_iota(jnp.int32, (WIDE, wide_cells), 1) // cells_n
        ).astype(F32) * scale
    ).astype(BF16)
    head_of = lax.broadcasted_iota(jnp.int32, (cells_n, WIDE), 1) // HD
    places = [[(k * shard + g * part_lanes, k) for k in range(quarter)] for g in range(groups)]

    def take(ref, g):
        return jnp.concatenate([ref[:, at : at + part_lanes] for at, _ in places[g]], axis=1)

    def by_head(value):
        total = value[:cells_n]
        for head in range(1, heads):
            total = jnp.where(head_of == head, value[head * cells_n : (head + 1) * cells_n], total)
        return total

    def attend(g):
        def both(ref, factor):
            value = take(ref, g).astype(F32) * factor
            return jnp.where(same_head, jnp.concatenate([value] * heads, axis=0), 0.0).astype(BF16)

        key_wide, value_wide, value_scaled = both(r.keys, 1.0), both(r.values, 1.0), both(r.values, scale)
        queries, douts = take(query, g), take(dout, g)
        expons = jnp.exp2(contract(queries, key_wide, 1, 1) * (scale * LOG2E))
        sums = contract(expons.astype(BF16), cell_ones, 1, 0)
        probabilities = expons / sums
        weights = probabilities.astype(BF16)
        got = contract(weights, value_wide, 1, 0).astype(BF16)
        r.att[g] = got
        grad_probs = contract(douts, value_scaled, 1, 1)
        deltas = contract((douts.astype(F32) * got.astype(F32)).astype(BF16), lane_ones, 1, 0)
        grad_scores = (probabilities * (grad_probs - deltas)).astype(BF16)
        grad_queries = contract(grad_scores, key_wide, 1, 0).astype(BF16)
        for at, k in places[g]:
            piece = grad_queries[:, k * part_lanes : (k + 1) * part_lanes]
            grad_query[:, at : at + part_lanes] = piece
            r.gq_split[g, k % 2, k // 2] = piece
        to_mate(r.gq_split.at[g, 1 - core], r.gq_in.at[g], 2 + g).start()
        to_mate(r.att.at[g], r.att_in.at[g], 2 + groups + g).start()
        grad_key = by_head(contract(grad_scores, queries, 0, 0))
        grad_value = by_head(contract(weights, douts, 0, 0))
        for owner in range(cols_n):
            rows = slice(owner * own, (owner + 1) * own)
            both_rows = jnp.concatenate([grad_key[rows], grad_value[rows]], axis=0).astype(BF16)
            for at, k in places[g]:
                r.blocks[owner, :, at : at + part_lanes] = both_rows[:, k * part_lanes : (k + 1) * part_lanes]

    def block(step):
        owner = col_mate(step)
        return remote(
            r.blocks.at[owner], r.blocks_in.at[step - 1], r.block_send.at[step - 1], r.block_recv.at[step - 1], row, owner
        )

    KINDS = (0, 1)
    made = (r.terms_q, r.terms_o)
    landed = (r.landed_q, r.landed_o)
    held = (r.held_q, r.held_o)
    line = (r.line_q, r.line_o)
    fin = (r.fin_q, r.fin_o)

    def terms(g):
        to_mate(r.gq_split.at[g, 1 - core], r.gq_in.at[g], 2 + g).wait()
        to_mate(r.att.at[g], r.att_in.at[g], 2 + groups + g).wait()
        for item in range(half):
            for_query = contract(hidden[...], r.gq_split[g, core, item], 0, 0) + contract(
                r.hidden_in[...], r.gq_in[g, item], 0, 0
            )
            for_out = contract(r.att[g], r.go_split[core, item], 0, 0) + contract(
                r.att_in[g], r.go_in[item], 0, 0
            )
            for kind, value in enumerate((for_query, for_out)):
                value = value.astype(BF16)
                size = value.shape[0] // rows_n
                for at in range(rows_n):
                    made[kind][g, item, position(at)] = value[at * size : (at + 1) * size]

    def halving(g, kind, item, step):
        count = rows_n >> (step + 1)
        base = made[kind] if step == 0 else held[kind]
        offset = rows_n - 2 * count
        number = kind * half + item
        return remote(
            base.at[g, item, pl.ds(count, count)], landed[kind].at[g, item, pl.ds(offset, count)],
            r.half_send.at[g, number, step], r.half_recv.at[g, number, step], row_partner(step), col,
        )

    paired = groups - 1
    parity = lax.rem(chip, 2)

    def kept(g, body):
        for kind in KINDS:
            if g == paired:
                pl.when(parity == kind)(partial(body, kind))
            else:
                body(kind)

    def pair(kind):
        return remote(
            made[kind].at[paired], (r.pair_q, r.pair_o)[kind], r.pair_sems.at[0], r.pair_sems.at[1],
            row, 2 * (chip + 1 - 2 * parity) + core,
        )

    def pair_start():
        kept(paired, lambda kind: pair(1 - kind).start())

    def pair_finish():
        def body(kind):
            pair(kind).wait_recv()
            for item in range(half):
                made[kind][paired, item] = (
                    made[kind][paired, item].astype(F32) + (r.pair_q, r.pair_o)[kind][item].astype(F32)
                ).astype(BF16)
            pair(1 - kind).wait_send()

        kept(paired, body)
        halve_start(paired)

    def halve_start(g):
        def body(kind):
            for item in range(half):
                halving(g, kind, item, 0).start()

        kept(g, body)

    def halve_finish(g, step):
        count = rows_n >> (step + 1)
        offset = rows_n - 2 * count

        def body(kind):
            for item in range(half):
                halving(g, kind, item, step).wait()
                base = made[kind] if step == 0 else held[kind]
                held[kind][g, item, 0:count] = (
                    base[g, item, 0:count].astype(F32)
                    + landed[kind][g, item, offset : offset + count].astype(F32)
                ).astype(BF16)
                if step < steps - 1:
                    halving(g, kind, item, step + 1).start()
                else:
                    @pl.when(chip != owner_of(kind, item))
                    def _(item=item):
                        along(g, kind, item).start()

                    @pl.when(chip == owner_of(kind, item))
                    def _(item=item):
                        line[kind][g, chip] = held[kind][g, item, 0]

        kept(g, body)

    def owner_of(kind, item):
        return item if kind == 0 else chips - half + item

    def along(g, kind, item):
        number = kind * half + item
        return remote(
            held[kind].at[g, item, 0], line[kind].at[g, chip],
            r.line_send.at[g, number], r.line_recv.at[g, chip], row, 2 * owner_of(kind, item) + core,
        )

    def arrived(g, kind, source):
        return remote(
            held[kind].at[g, 0, 0], line[kind].at[g, source],
            r.line_send.at[g, 0], r.line_recv.at[g, source], row, 2 * source + core,
        )

    def spread_out(g, kind, step):
        return remote(
            fin[kind].at[g, row], fin[kind].at[g, row],
            r.spread_send.at[g, step - 1], r.spread_recv.at[g, step - 1], row_mate(step), col,
        )

    def each_owner(body):
        for kind, here, item in ((0, is_query, chip), (1, is_out, chip - (chips - half))):
            @pl.when(here)
            def _(kind=kind, item=item):
                body(kind, item)

    def line_finish(g):
        def body(kind, item):
            total = None
            for source in range(kind, chips, 2) if g == paired else range(chips):
                @pl.when(chip != source)
                def _(source=source):
                    arrived(g, kind, source).wait_recv()

                value = line[kind][g, source].astype(F32)
                total = value if total is None else total + value
            fin[kind][g, row] = total.astype(BF16)
            for step in range(1, rows_n):
                spread_out(g, kind, step).start()

        each_owner(body)

    def place_final(g):
        def body(kind, item):
            for step in range(1, rows_n):
                spread_out(g, kind, step).wait()
            for part in range(rows_n):
                value = fin[kind][g, part].astype(F32)
                if kind == 0:
                    size = channels // rows_n
                    r.grad_weights[part * size : (part + 1) * size, g * part_lanes : (g + 1) * part_lanes] = value
                else:
                    size = WIDE // rows_n
                    k = (part * size) // part_lanes
                    at = k * shard + g * part_lanes + part * size - k * part_lanes
                    r.grad_weights[at : at + size] = value

        each_owner(body)

    go_copy.wait()
    hidden_copy.wait()
    for g in range(groups):
        attend(g)
    for step in range(1, cols_n):
        block(step).start()
    for g in range(groups):
        terms(g)
        if g == paired:
            pair_start()
        else:
            halve_start(g)

    @pl.loop(0, 2)
    def _(at):
        rows = chunk_of(at)
        value = contract(grad_query[rows], r.w_query_v[...], 1, 1) + grad_out[rows].astype(F32)
        pad2[pl.ds(1 + at * (height // 2), height // 2)] = value.reshape(height // 2, width, channels)

    halve_finish(0, 0)

    for at in range(height):
        for which, value in enumerate((pad2[at + 1, 0:1], pad2[at + 1, width - 1 : width])):
            r.stage1[which, at : at + 1] = value
    r.tap_terms[...] = jnp.zeros_like(r.tap_terms)

    @pl.loop(0, parts)
    def _(part):
        lanes = lanes_of(part)
        sums = [jnp.zeros((8, LANES), F32) for _ in range(9)]
        for at in range(height):
            value = pad2[at + 1, :, lanes]
            shifted = [from_right(value, 0.0), value, from_left(value, 0.0)]
            for a in range(3):
                x = pad1[at + a, :, lanes]
                for b in range(3):
                    sums[3 * a + b] = sums[3 * a + b] + (shifted[b] * x).reshape(width // 8, 8, LANES).sum(axis=0)
        for i in range(9):
            total = sums[i].sum(axis=0, keepdims=True)
            if i % 3 != 1:
                which = 0 if i % 3 == 0 else 1
                product = r.stage1[which, :, lanes] * r.side1[which, i // 3 : i // 3 + height, lanes]
                total = total + product.sum(axis=0, keepdims=True)
            r.tap_terms[i : i + 1, lanes] = total

    totals = r.blocks[col].astype(F32)
    for step in range(1, cols_n):
        block(step).wait()
        totals = totals + r.blocks_in[step - 1].astype(F32)
    high, low = split(totals)
    tot_all = r.tot_all
    tot_all[col] = high

    def tot(target):
        return remote(
            tot_all.at[col], tot_all.at[col], r.tot_send.at[target - quarter], r.tot_recv.at[col], row, target
        )

    def tot_from(source):
        return remote(
            tot_all.at[source], tot_all.at[source], r.tot_send.at[0], r.tot_recv.at[source], row, source
        )

    for target in range(quarter, 3 * quarter):
        @pl.when(col != target)
        def _(target=target):
            tot(target).start()

    both_parts = jnp.concatenate([high, low], axis=0)
    by_key = contract(both_parts, r.w_key_v[...], 1, 1)
    by_value = contract(both_parts, r.w_value_v[...], 1, 1)
    grad_normed = by_key[:own] + by_key[2 * own : 3 * own] + by_value[own : 2 * own] + by_value[3 * own :]
    grad_pooled = (
        grad_normed
        - jnp.mean(grad_normed, axis=-1, keepdims=True)
        - standard * jnp.mean(grad_normed * standard, axis=-1, keepdims=True)
    ) * (inverse / (POOL * POOL))
    r.grad_pooled[...] = grad_pooled
    narrow = channels // cols_n
    for i in range(9):
        r.tap_terms[i : i + 1] = r.tap_terms[i : i + 1] + (r.windows[i] * grad_pooled).sum(axis=0, keepdims=True)
    for at in range(cols_n):
        r.tap_out[at] = r.tap_terms[:, at * narrow : (at + 1) * narrow].astype(BF16)

    def tap_first(step):
        return remote(
            r.tap_out.at[col_mate(step)], r.tap_in.at[step - 1],
            r.tap_send1.at[step - 1], r.tap_recv1.at[step - 1], row, col_mate(step),
        )

    def tap_second(step):
        return remote(
            r.tap_out2, r.tap_in2.at[step - 1], r.tap_send2.at[step - 1], r.tap_recv2.at[step - 1], row_mate(step), col
        )

    for step in range(1, cols_n):
        tap_first(step).start()

    for g in range(1, groups - 1):
        halve_finish(g, 0)
    pair_finish()

    @pl.loop(0, parts)
    def _(part):
        lanes = lanes_of(part)
        for cell_row in range(height // POOL):
            over = jnp.concatenate(
                [
                    jnp.broadcast_to(r.grad_pooled[at : at + 1, lanes], (POOL, LANES))
                    for at in range(cell_row * per_row, (cell_row + 1) * per_row)
                ],
                axis=0,
            )
            for at in range(cell_row * POOL, (cell_row + 1) * POOL):
                value = pad2[at + 1, :, lanes] + over
                pad2[at + 1, :, lanes] = value
                if at == 0 or at == height - 1:
                    r.rows_out2[0 if at == 0 else 1, :, lanes] = value.astype(BF16)

    pack_edges(halo2, lambda at: pad2[at + 1, 0:1], lambda at: pad2[at + 1, width - 1 : width])
    send_halo(halo2, range(8))

    for g in range(groups - 1):
        for step in range(1, steps):
            halve_finish(g, step)
    halve_finish(paired, 0)

    @pl.when(is_cells)
    def _():
        for step in range(1, cols_n):
            tot_from(col_mate(step)).wait_recv()
        is_key = col < 2 * quarter
        sides = []
        for at in range(cols_n):
            value = tot_all[at].astype(F32)
            sides.append(jnp.where(is_key, value[:own], value[own:]))
        value = jnp.concatenate(sides, axis=0)
        mine = value[:, :shard]
        for k in range(1, quarter):
            mine = jnp.where(lax.rem(col, quarter) == k, value[:, k * shard : (k + 1) * shard], mine)
        r.side_all[row] = mine.astype(BF16)
        for step in range(1, rows_n):
            pass_on(r.side_all, 1, step).start()

    tap_total = r.tap_out[col].astype(F32)
    for step in range(1, cols_n):
        tap_first(step).wait()
        tap_total = tap_total + r.tap_in[step - 1].astype(F32)
    r.tap_out2[...] = tap_total.astype(BF16)
    for step in range(1, rows_n):
        tap_second(step).start()

    for step in range(1, steps):
        halve_finish(groups - 1, step)
    for g in range(groups):
        line_finish(g)
    wait_halo(halo2)
    take_halo(halo2)

    @pl.loop(0, parts)
    def _(part):
        lanes = lanes_of(part)
        w = weights_of(lanes)
        short = [jnp.broadcast_to(taps[i : i + 1, lanes], (height, LANES)) for i in range(9)]
        for which in range(2):
            total = jnp.zeros((height, LANES), F32)
            for a in range(3):
                total = total + short[3 * a + 2 - 2 * which] * r.side2[which, 2 - a : 2 - a + height, lanes]
            r.edge_sum[which, :, lanes] = total
        for at in range(height):
            x = [pad2[at + 2 - a, :, lanes] for a in range(3)]
            sums = [w[b] * x[0] + w[3 + b] * x[1] + w[6 + b] * x[2] for b in range(3)]
            total = (
                sums[1]
                + from_right(sums[0], r.edge_sum[1, at : at + 1, lanes])
                + from_left(sums[2], r.edge_sum[0, at : at + 1, lanes])
            )
            r.grad_image[at, :, lanes] = total.astype(BF16)

    @pl.when(is_cells)
    def _():
        for at, ref in enumerate((r.key_all, r.side_all)):
            for step in range(1, rows_n):
                pass_on(ref, at, step).wait()
        keys = r.key_all[...].reshape(rows_n * cells_n, channels)
        sides = r.side_all[...].reshape(rows_n * cells_n, shard)
        r.grad_weights[...] = contract(keys, sides, 0, 0)

    tap_total = r.tap_out2[...].astype(F32)
    for step in range(1, rows_n):
        tap_second(step).wait()
        tap_total = tap_total + r.tap_in2[step - 1].astype(F32)
    r.grad_conv[...] = tap_total[:9]

    for g in range(groups):
        place_final(g)

    for target in range(quarter, 3 * quarter):
        @pl.when(col != target)
        def _(target=target):
            tot(target).wait_send()
    def drain(g, kind):
        for item in range(half):
            @pl.when(chip != owner_of(kind, item))
            def _(item=item):
                along(g, kind, item).wait_send()

    for g in range(groups):
        kept(g, partial(drain, g))


def store_kernel(count, *refs):
    copies = [pltpu.make_async_copy(refs[at], refs[count + at], refs[2 * count].at[at]) for at in range(count)]
    for copy in copies:
        copy.start()
    for copy in copies:
        copy.wait()


def on_device(image, conv_taps, w_query, w_key, w_value, w_out, grad_out):
    rows_n, cols_n = lax.axis_size("row"), lax.axis_size("col")
    height, width, channels = image.shape
    tokens = height * width
    own = (height // POOL) * (width // POOL)
    cells_n = cols_n * own
    chips, quarter = cols_n // 2, cols_n // 4
    half = quarter // 2
    shard = 4 * channels // cols_n
    groups = channels // WIDE
    part_lanes = shard // groups
    steps = bits_of(rows_n)
    part_q, part_o = (channels // rows_n, part_lanes), (WIDE // rows_n, shard)
    operands = dict(
        image=image, grad_out=grad_out.reshape(tokens, channels), taps=conv_taps,
        w_query=w_query, w_key=w_key, w_value=w_value, w_out=w_out,
    )
    outputs = dict(
        grad_image=(image.shape, BF16),
        grad_weights=((channels, shard), F32),
        grad_conv=((9, channels // cols_n), F32),
    )
    square = ((channels, channels), BF16)
    flat = ((tokens, channels), BF16)
    edge_cols, edge_rows = ((2, height, channels), BF16), ((2, width, channels), BF16)
    corner = ((4, 8, channels), F32)
    scratch = dict(
        image_v=(image.shape, BF16), grad_out_v=flat, taps_v=(conv_taps.shape, F32),
        w_query_v=square, w_key_v=square, w_value_v=square, w_out_v=square,
        pad1=((height + 2, width, channels), F32), pad2=((height + 2, width, channels), F32),
        stage1=((2, height, channels), F32), stage2=((2, height, channels), F32),
        side1=((2, height + 8, channels), F32), side2=((2, height + 8, channels), F32),
        edge_sum=((2, height, channels), F32), mixed=((height, width, channels), F32),
        windows=((9, own, channels), F32),
        rows_out2=edge_rows,
        hidden=flat, query=flat, dout=flat, grad_query=flat, hidden_in=flat,
        go_split=((2, half, tokens, shard), BF16), go_in=((half, tokens, shard), BF16),
        gq_split=((groups, 2, half, tokens, part_lanes), BF16), gq_in=((groups, half, tokens, part_lanes), BF16),
        att=((groups, tokens, WIDE), BF16), att_in=((groups, tokens, WIDE), BF16),
        pooled=((own, channels), F32), grad_pooled=((own, channels), F32),
        cellbuf=((cols_n, own, channels), BF16),
        keys=((cells_n, channels), BF16), values=((cells_n, channels), BF16),
        key_all=((rows_n, cells_n, channels), BF16), side_all=((rows_n, cells_n, shard), BF16),
        blocks=((cols_n, 2 * own, channels), BF16), blocks_in=((cols_n - 1, 2 * own, channels), BF16),
        tot_all=((cols_n, 2 * own, channels), BF16),
        cols_out1=edge_cols, cols_in1=edge_cols, rows_in1=edge_rows, corners_in1=corner, corners_out1=corner,
        cols_out2=edge_cols, cols_in2=edge_cols, rows_in2=edge_rows, corners_in2=corner, corners_out2=corner,
        terms_q=((groups, half, rows_n) + part_q, BF16), terms_o=((groups, half, rows_n) + part_o, BF16),
        landed_q=((groups, half, rows_n - 1) + part_q, BF16), landed_o=((groups, half, rows_n - 1) + part_o, BF16),
        held_q=((groups, half, rows_n // 2) + part_q, BF16), held_o=((groups, half, rows_n // 2) + part_o, BF16),
        line_q=((groups, chips) + part_q, BF16), line_o=((groups, chips) + part_o, BF16),
        fin_q=((groups, rows_n) + part_q, BF16), fin_o=((groups, rows_n) + part_o, BF16),
        pair_q=((half, rows_n) + part_q, BF16), pair_o=((half, rows_n) + part_o, BF16),
        tap_terms=((16, channels), F32),
        tap_out=((cols_n, 16, channels // cols_n), BF16), tap_in=((cols_n - 1, 16, channels // cols_n), BF16),
        tap_out2=((16, channels // cols_n), BF16), tap_in2=((rows_n - 1, 16, channels // cols_n), BF16),
    )
    sems = dict(
        loaded=(7,), pair_sems=(2,),
        halo_send1=(8,), halo_recv1=(8,), halo_send2=(8,), halo_recv2=(8,),
        mate_send=(2 + 2 * groups,), mate_recv=(2 + 2 * groups,),
        cell_send=(cols_n - 1,), cell_recv=(cols_n - 1,),
        block_send=(cols_n - 1,), block_recv=(cols_n - 1,),
        tot_send=(2 * quarter,), tot_recv=(cols_n,),
        half_send=(groups, 2 * half, steps), half_recv=(groups, 2 * half, steps),
        line_send=(groups, 2 * half), line_recv=(groups, chips),
        spread_send=(groups, rows_n - 1), spread_recv=(groups, rows_n - 1),
        tap_send1=(cols_n - 1,), tap_recv1=(cols_n - 1,),
        tap_send2=(rows_n - 1,), tap_recv2=(rows_n - 1,),
        pass_send=(2, rows_n - 1), pass_recv=(2, rows_n - 1),
    )
    names = list(operands) + list(outputs) + list(scratch) + list(sems)
    made = pl.pallas_call(
        partial(block_kernel, rows_n, cols_n, names),
        out_shape=[pltpu.VMEM(*spec) for spec in outputs.values()],
        in_specs=[HBM] * len(operands),
        out_specs=[pl.BlockSpec(memory_space=pltpu.VMEM)] * len(outputs),
        scratch_shapes=[pltpu.VMEM(*spec) for spec in scratch.values()]
        + [pltpu.SemaphoreType.DMA(spec) for spec in sems.values()],
        compiler_params=pltpu.CompilerParams(
            collective_id=0, has_side_effects=True, vmem_limit_bytes=48 * 2**20
        ),
    )(*[pltpu.with_memory_space_constraint(value, pltpu.HBM) for value in operands.values()])
    return tuple(
        pl.pallas_call(
            partial(store_kernel, len(outputs)),
            out_shape=[pltpu.HBM(*spec) for spec in outputs.values()],
            in_specs=[pl.BlockSpec(memory_space=pltpu.VMEM)] * len(outputs),
            out_specs=[HBM] * len(outputs),
            scratch_shapes=[pltpu.SemaphoreType.DMA((len(outputs),))],
        )(*[pltpu.with_memory_space_constraint(value, pltpu.VMEM) for value in made])
    )


def solution(mesh):
    return jax.shard_map(
        on_device,
        mesh=mesh,
        in_specs=(P("row", "col", None), P(), P(), P(), P(), P(), P("row", "col", None)),
        out_specs=(P("row", "col", None), P(None, "col"), P(None, "col")),
        check_vma=False,
    )
```

```python
from functools import partial
from types import SimpleNamespace

import jax
import jax.numpy as jnp
from jax import lax
from jax.experimental import pallas as pl
from jax.experimental.pallas import tpu as pltpu
from jax.sharding import PartitionSpec as P

HD = 64
POOL = 8
LANES = 128
WIDE = 256
EDGE = 16

EPSILON = 1e-05
LOG2E = 1.4426950408889634
MESH = pl.DeviceIdType.MESH
HBM = pl.BlockSpec(memory_space=pltpu.HBM)
DIRECTIONS = ((-1, -1), (-1, 1), (1, -1), (1, 1), (-1, 0), (1, 0), (0, -1), (0, 1))
CORNERS = (0, 1, 2, 3)
ROWS = (4, 5)
COLUMNS = (6, 7)
F32 = jnp.float32
BF16 = jnp.bfloat16


def contract(left, right, at_left, at_right):
    return lax.dot_general(
        left, right, (((at_left,), (at_right,)), ((), ())), preferred_element_type=F32
    )


def split(value):
    high = value.astype(BF16)
    return high, (value - high.astype(F32)).astype(BF16)


def remote(source, target, send, recv, row, col):
    return pltpu.make_async_remote_copy(
        src_ref=source,
        dst_ref=target,
        send_sem=send,
        recv_sem=recv,
        device_id=(row, col),
        device_id_type=MESH,
    )


def bits_of(count):
    return count.bit_length() - 1


def flip(row, bit):
    size = 2**bit
    return row + size * (1 - 2 * lax.rem(row // size, 2))


def block_kernel(rows_n, cols_n, names, *refs):
    r = SimpleNamespace(**dict(zip(names, refs, strict=True)))
    image, grad_out, taps = r.image_v, r.grad_out_v, r.taps_v
    pad1, pad2 = r.pad1, r.pad2
    hidden, query, dout = r.hidden, r.query, r.dout
    grad_query = r.grad_query
    height, width, channels = image.shape
    tokens = height * width
    own = (height // POOL) * (width // POOL)
    per_row = width // POOL
    cells_n = cols_n * own
    shard = 4 * channels // cols_n
    quarter = cols_n // 4
    half = quarter // 2
    groups = channels // WIDE
    part_lanes = shard // groups
    steps = bits_of(rows_n)
    parts = channels // LANES
    row, col = lax.axis_index("row"), lax.axis_index("col")
    chip, core = col // 2, lax.rem(col, 2)
    chips = cols_n // 2
    is_query = chip < half
    is_out = chip >= chips - half
    is_cells = jnp.logical_and(chip >= half, chip < chips - half)

    def row_mate(step):
        return lax.rem(row + step, rows_n)

    def col_mate(step):
        return lax.rem(col + step, cols_n)

    def row_partner(step):
        return (1 - core) * flip(row, step) + core * flip(row, steps - 1 - step)

    def position(of):
        def by(order):
            at = 0
            for step, bit in enumerate(order):
                size = 2**bit
                at = at + lax.rem(row // size + of // size, 2) * 2 ** (steps - 1 - step)
            return at

        return (1 - core) * by(range(steps)) + core * by(range(steps - 1, -1, -1))

    def present(down, right):
        ok = None
        for move, at, count in ((down, row, rows_n), (right, col, cols_n)):
            if move == 0:
                continue
            here = at > 0 if move < 0 else at < count - 1
            ok = here if ok is None else jnp.logical_and(ok, here)
        return ok

    def load(source, target, at):
        return pltpu.make_async_copy(source, target, r.loaded.at[at])

    load_image, load_taps = load(r.image, image, 0), load(r.taps, taps, 1)
    load_grad_out, load_out = load(r.grad_out, grad_out, 2), load(r.w_out, r.w_out_v, 3)
    load_query, load_key = load(r.w_query, r.w_query_v, 4), load(r.w_key, r.w_key_v, 5)
    load_value = load(r.w_value, r.w_value_v, 6)
    load_image.start()
    load_taps.start()

    halo1 = SimpleNamespace(
        pad=pad1, stage=r.stage1, side=r.side1, cols_out=r.cols_out1, cols_in=r.cols_in1, rows_in=r.rows_in1,
        corners_out=r.corners_out1, corners_in=r.corners_in1, send=r.halo_send1, recv=r.halo_recv1,
        edge_rows=(r.image.at[0], r.image.at[height - 1]),
    )
    halo2 = SimpleNamespace(
        pad=pad2, stage=r.stage2, side=r.side2, cols_out=r.cols_out2, cols_in=r.cols_in2, rows_in=r.rows_in2,
        corners_out=r.corners_out2, corners_in=r.corners_in2, send=r.halo_send2, recv=r.halo_recv2,
        edge_rows=(r.rows_out2.at[0], r.rows_out2.at[1]),
    )
    for halo in (halo1, halo2):
        for ref in (halo.cols_in, halo.rows_in, halo.corners_in):
            ref[...] = jnp.zeros_like(ref)

    barrier = pltpu.get_barrier_semaphore()
    greeted = cols_n + rows_n - 2
    for down, right in DIRECTIONS[:4]:
        greeted = greeted + present(down, right).astype(jnp.int32)

        @pl.when(present(down, right))
        def _(down=down, right=right):
            pl.semaphore_signal(barrier, inc=1, device_id=(row + down, col + right), device_id_type=MESH)
    for step in range(1, cols_n):
        pl.semaphore_signal(barrier, inc=1, device_id=(row, col_mate(step)), device_id_type=MESH)
    for step in range(1, rows_n):
        pl.semaphore_signal(barrier, inc=1, device_id=(row_mate(step), col), device_id_type=MESH)

    def edge(halo, at):
        down, right = DIRECTIONS[at]
        edge_row = halo.edge_rows[0 if down < 0 else 1]
        if down == 0:
            source, target = halo.cols_out.at[0 if right < 0 else 1], halo.cols_in.at[1 if right < 0 else 0]
        elif right == 0:
            source, target = edge_row, halo.rows_in.at[1 if down < 0 else 0]
        else:
            source = halo.corners_out.at[(0 if down < 0 else 2) + (0 if right < 0 else 1), pl.ds(0, 1)]
            target = halo.corners_in.at[(2 if down < 0 else 0) + (1 if right < 0 else 0), pl.ds(0, 1)]
        return remote(source, target, halo.send.at[at], halo.recv.at[at], row + down, col + right)

    def pack_edges(halo, first, last):
        for at in range(height):
            for which, value in enumerate((first(at), last(at))):
                halo.stage[which, at : at + 1] = value
                if at == 0 or at == height - 1:
                    halo.corners_out[(0 if at == 0 else 2) + which, 0:1] = value
        halo.cols_out[...] = halo.stage[...].astype(BF16)

    def send_halo(halo, wanted):
        for at in wanted:
            down, right = DIRECTIONS[at]

            @pl.when(present(down, right))
            def _(at=at):
                edge(halo, at).start()

    def wait_halo(halo):
        for at, (down, right) in enumerate(DIRECTIONS):
            @pl.when(present(-down, -right))
            def _(at=at):
                edge(halo, at).wait_recv()

            @pl.when(present(down, right))
            def _(at=at):
                edge(halo, at).wait_send()

    def take_halo(halo):
        halo.pad[0] = halo.rows_in[0].astype(F32)
        halo.pad[height + 1] = halo.rows_in[1].astype(F32)
        for which in range(2):
            halo.side[which, 1 : height + 1] = halo.cols_in[which].astype(F32)
            halo.side[which, 0:1] = halo.corners_in[which, 0:1]
            halo.side[which, height + 1 : height + 2] = halo.corners_in[2 + which, 0:1]

    sublane = lax.broadcasted_iota(jnp.int32, (width, LANES), 0)
    first_column, last_column = sublane == 0, sublane == width - 1

    def from_left(value, halo):
        return jnp.where(first_column, halo, pltpu.roll(value, 1, 0))

    def from_right(value, halo):
        return jnp.where(last_column, halo, pltpu.roll(value, width - 1, 0))

    def lanes_of(part):
        return pl.ds(pl.multiple_of(part * LANES, LANES), LANES)

    pl.semaphore_wait(barrier, greeted)
    send_halo(halo1, ROWS)
    load_image.wait()
    for copy in (load_grad_out, load_out, load_query, load_key, load_value):
        copy.start()
    pack_edges(
        halo1,
        lambda at: image[at, :EDGE].astype(F32)[:1],
        lambda at: image[at, width - EDGE :].astype(F32)[EDGE - 1 :],
    )
    send_halo(halo1, CORNERS + COLUMNS)
    load_taps.wait()
    pad1[0] = jnp.zeros_like(pad1[0])
    pad1[height + 1] = jnp.zeros_like(pad1[0])

    @pl.loop(0, height)
    def _(at):
        pad1[at + 1] = image[at].astype(F32)

    def weights_of(lanes):
        w = [jnp.broadcast_to(taps[i : i + 1, lanes], (width, LANES)) for i in range(9)]
        w[4] = w[4] + 1.0
        return w

    @pl.loop(0, parts)
    def _(part):
        lanes = lanes_of(part)
        w = weights_of(lanes)
        for at in range(height):
            x = [pad1[at + a, :, lanes] for a in range(3)]
            sums = [w[b] * x[0] + w[3 + b] * x[1] + w[6 + b] * x[2] for b in range(3)]
            r.mixed[at, :, lanes] = sums[1] + from_left(sums[0], 0.0) + from_right(sums[2], 0.0)

    chunk = tokens // 2

    def chunk_of(at):
        return pl.ds(pl.multiple_of(at * chunk, chunk), chunk)

    load_grad_out.wait()
    load_out.wait()

    @pl.loop(0, 2)
    def _(at):
        rows = chunk_of(at)
        dout[rows] = contract(grad_out[rows], r.w_out_v[...], 1, 1).astype(BF16)

    for side in range(2):
        for item in range(half):
            at = (2 * item + side) * shard
            r.go_split[side, item] = grad_out[:, at : at + shard]

    def to_mate(source, target, at):
        return remote(source, target, r.mate_send.at[at], r.mate_recv.at[at], row, 2 * chip + 1 - core)

    go_copy = to_mate(r.go_split.at[1 - core], r.go_in, 0)
    go_copy.start()
    wait_halo(halo1)
    take_halo(halo1)

    edge_sublane = lax.broadcasted_iota(jnp.int32, (8, LANES), 0)

    @pl.loop(0, parts)
    def _(part):
        lanes = lanes_of(part)
        w = [jnp.broadcast_to(taps[i : i + 1, lanes], (width, LANES)) for i in range(9)]
        short = [jnp.broadcast_to(taps[i : i + 1, lanes], (height, LANES)) for i in range(9)]
        for which in range(2):
            total = jnp.zeros((height, LANES), F32)
            for a in range(3):
                total = total + short[3 * a + 2 * which] * r.side1[which, a : a + height, lanes]
            r.edge_sum[which, :, lanes] = total
        for cell_row in range(height // POOL):
            pooled = jnp.zeros((width, LANES), F32)
            for at in range(cell_row * POOL, (cell_row + 1) * POOL):
                total = r.mixed[at, :, lanes]
                for edge_at, a in ((0, 0), (height - 1, 2)):
                    if at == edge_at:
                        x = pad1[at + a, :, lanes]
                        total = (
                            total + w[3 * a + 1] * x + from_left(w[3 * a] * x, 0.0) + from_right(w[3 * a + 2] * x, 0.0)
                        )
                left = jnp.where(edge_sublane == 0, r.edge_sum[0, at : at + 1, lanes], 0.0)
                right = jnp.where(edge_sublane == 7, r.edge_sum[1, at : at + 1, lanes], 0.0)
                total = jnp.concatenate(
                    [total[:8] + left, total[8 : width - 8], total[width - 8 :] + right], axis=0
                )
                value = total.astype(BF16)
                hidden[at * width : (at + 1) * width, lanes] = value
                pooled = pooled + value.astype(F32)
            where = slice(cell_row * per_row, (cell_row + 1) * per_row)
            r.pooled[where, lanes] = pooled.reshape(per_row, POOL, LANES).sum(axis=1) / (POOL * POOL)

    pooled = r.pooled[...]
    centre = jnp.mean(pooled, axis=-1, keepdims=True)
    spread = jnp.mean(jnp.square(pooled - centre), axis=-1, keepdims=True)
    inverse = lax.rsqrt(spread + EPSILON)
    standard = (pooled - centre) * inverse
    cellbuf = r.cellbuf
    cellbuf[col] = standard.astype(BF16)

    def cell(step):
        return remote(
            cellbuf.at[col], cellbuf.at[col], r.cell_send.at[step - 1], r.cell_recv.at[step - 1], row, col_mate(step)
        )

    for step in range(1, cols_n):
        cell(step).start()
    hidden_copy = to_mate(hidden, r.hidden_in, 1)
    hidden_copy.start()

    load_query.wait()

    @pl.loop(0, 2)
    def _(at):
        rows = chunk_of(at)
        query[rows] = contract(hidden[rows], r.w_query_v[...], 1, 0).astype(BF16)

    @pl.loop(0, parts)
    def _(part):
        lanes = lanes_of(part)
        for cell_row in range(height // POOL):
            for a in range(3):
                first = cell_row * POOL + a
                total = pad1[first, :, lanes]
                for at in range(first + 1, first + POOL):
                    total = total + pad1[at, :, lanes]
                left, right = (
                    r.side1[which, first : first + POOL, lanes].sum(axis=0, keepdims=True) for which in range(2)
                )
                for b, value in enumerate((from_left(total, left), total, from_right(total, right))):
                    r.windows[3 * a + b, cell_row * per_row : (cell_row + 1) * per_row, lanes] = value.reshape(
                        per_row, POOL, LANES
                    ).sum(axis=1)

    load_key.wait()
    load_value.wait()
    for step in range(1, cols_n):
        cell(step).wait()
    key_cells = jnp.concatenate([cellbuf[at].astype(F32) for at in range(cols_n)], axis=0).astype(BF16)
    r.key_all[row] = key_cells

    def pass_on(ref, at, step):
        return remote(
            ref.at[row], ref.at[row], r.pass_send.at[at, step - 1], r.pass_recv.at[at, step - 1], row_mate(step), col
        )

    @pl.when(is_cells)
    def _():
        for step in range(1, rows_n):
            pass_on(r.key_all, 0, step).start()

    r.keys[...] = contract(key_cells, r.w_key_v[...], 1, 0).astype(BF16)
    r.values[...] = contract(key_cells, r.w_value_v[...], 1, 0).astype(BF16)

    heads = WIDE // HD
    wide_cells = heads * cells_n
    same_head = (
        lax.broadcasted_iota(jnp.int32, (wide_cells, WIDE), 0) // cells_n
        == lax.broadcasted_iota(jnp.int32, (wide_cells, WIDE), 1) // HD
    )
    cell_ones = (
        lax.broadcasted_iota(jnp.int32, (wide_cells, wide_cells), 0) // cells_n
        == lax.broadcasted_iota(jnp.int32, (wide_cells, wide_cells), 1) // cells_n
    ).astype(F32).astype(BF16)
    scale = HD ** (-0.5)
    lane_ones = (
        (
            lax.broadcasted_iota(jnp.int32, (WIDE, wide_cells), 0) // HD
            == lax.broadcasted_iota(jnp.int32, (WIDE, wide_cells), 1) // cells_n
        ).astype(F32) * scale
    ).astype(BF16)
    head_of = lax.broadcasted_iota(jnp.int32, (cells_n, WIDE), 1) // HD
    places = [[(k * shard + g * part_lanes, k) for k in range(quarter)] for g in range(groups)]

    def take(ref, g):
        return jnp.concatenate([ref[:, at : at + part_lanes] for at, _ in places[g]], axis=1)

    def by_head(value):
        total = value[:cells_n]
        for head in range(1, heads):
            total = jnp.where(head_of == head, value[head * cells_n : (head + 1) * cells_n], total)
        return total

    def attend(g):
        def both(ref, factor):
            value = take(ref, g).astype(F32) * factor
            return jnp.where(same_head, jnp.concatenate([value] * heads, axis=0), 0.0).astype(BF16)

        key_wide, value_wide, value_scaled = both(r.keys, 1.0), both(r.values, 1.0), both(r.values, scale)
        queries, douts = take(query, g), take(dout, g)
        expons = jnp.exp2(contract(queries, key_wide, 1, 1) * (scale * LOG2E))
        sums = contract(expons.astype(BF16), cell_ones, 1, 0)
        probabilities = expons / sums
        weights = probabilities.astype(BF16)
        got = contract(weights, value_wide, 1, 0).astype(BF16)
        r.att[g] = got
        grad_probs = contract(douts, value_scaled, 1, 1)
        deltas = contract((douts.astype(F32) * got.astype(F32)).astype(BF16), lane_ones, 1, 0)
        grad_scores = (probabilities * (grad_probs - deltas)).astype(BF16)
        grad_queries = contract(grad_scores, key_wide, 1, 0).astype(BF16)
        for at, k in places[g]:
            piece = grad_queries[:, k * part_lanes : (k + 1) * part_lanes]
            grad_query[:, at : at + part_lanes] = piece
            r.gq_split[g, k % 2, k // 2] = piece
        to_mate(r.gq_split.at[g, 1 - core], r.gq_in.at[g], 2 + g).start()
        to_mate(r.att.at[g], r.att_in.at[g], 2 + groups + g).start()
        grad_key = by_head(contract(grad_scores, queries, 0, 0))
        grad_value = by_head(contract(weights, douts, 0, 0))
        for owner in range(cols_n):
            rows = slice(owner * own, (owner + 1) * own)
            both_rows = jnp.concatenate([grad_key[rows], grad_value[rows]], axis=0).astype(BF16)
            for at, k in places[g]:
                r.blocks[owner, :, at : at + part_lanes] = both_rows[:, k * part_lanes : (k + 1) * part_lanes]

    def block(step):
        owner = col_mate(step)
        return remote(
            r.blocks.at[owner], r.blocks_in.at[step - 1], r.block_send.at[step - 1], r.block_recv.at[step - 1], row, owner
        )

    KINDS = (0, 1)
    made = (r.terms_q, r.terms_o)
    landed = (r.landed_q, r.landed_o)
    held = (r.held_q, r.held_o)
    line = (r.line_q, r.line_o)
    fin = (r.fin_q, r.fin_o)

    def terms(g):
        to_mate(r.gq_split.at[g, 1 - core], r.gq_in.at[g], 2 + g).wait()
        to_mate(r.att.at[g], r.att_in.at[g], 2 + groups + g).wait()
        for item in range(half):
            for_query = contract(hidden[...], r.gq_split[g, core, item], 0, 0) + contract(
                r.hidden_in[...], r.gq_in[g, item], 0, 0
            )
            for_out = contract(r.att[g], r.go_split[core, item], 0, 0) + contract(
                r.att_in[g], r.go_in[item], 0, 0
            )
            for kind, value in enumerate((for_query, for_out)):
                value = value.astype(BF16)
                size = value.shape[0] // rows_n
                for at in range(rows_n):
                    made[kind][g, item, position(at)] = value[at * size : (at + 1) * size]

    def halving(g, kind, item, step):
        count = rows_n >> (step + 1)
        base = made[kind] if step == 0 else held[kind]
        offset = rows_n - 2 * count
        number = kind * half + item
        return remote(
            base.at[g, item, pl.ds(count, count)], landed[kind].at[g, item, pl.ds(offset, count)],
            r.half_send.at[g, number, step], r.half_recv.at[g, number, step], row_partner(step), col,
        )

    paired = groups - 1
    parity = lax.rem(chip, 2)

    def kept(g, body):
        for kind in KINDS:
            if g == paired:
                pl.when(parity == kind)(partial(body, kind))
            else:
                body(kind)

    def pair(kind):
        return remote(
            made[kind].at[paired], (r.pair_q, r.pair_o)[kind], r.pair_sems.at[0], r.pair_sems.at[1],
            row, 2 * (chip + 1 - 2 * parity) + core,
        )

    def pair_start():
        kept(paired, lambda kind: pair(1 - kind).start())

    def pair_finish():
        def body(kind):
            pair(kind).wait_recv()
            for item in range(half):
                made[kind][paired, item] = (
                    made[kind][paired, item].astype(F32) + (r.pair_q, r.pair_o)[kind][item].astype(F32)
                ).astype(BF16)
            pair(1 - kind).wait_send()

        kept(paired, body)
        halve_start(paired)

    def halve_start(g):
        def body(kind):
            for item in range(half):
                halving(g, kind, item, 0).start()

        kept(g, body)

    def halve_finish(g, step):
        count = rows_n >> (step + 1)
        offset = rows_n - 2 * count

        def body(kind):
            for item in range(half):
                halving(g, kind, item, step).wait()
                base = made[kind] if step == 0 else held[kind]
                held[kind][g, item, 0:count] = (
                    base[g, item, 0:count].astype(F32)
                    + landed[kind][g, item, offset : offset + count].astype(F32)
                ).astype(BF16)
                if step < steps - 1:
                    halving(g, kind, item, step + 1).start()
                else:
                    @pl.when(chip != owner_of(kind, item))
                    def _(item=item):
                        along(g, kind, item).start()

                    @pl.when(chip == owner_of(kind, item))
                    def _(item=item):
                        line[kind][g, chip] = held[kind][g, item, 0]

        kept(g, body)

    def owner_of(kind, item):
        return item if kind == 0 else chips - half + item

    def along(g, kind, item):
        number = kind * half + item
        return remote(
            held[kind].at[g, item, 0], line[kind].at[g, chip],
            r.line_send.at[g, number], r.line_recv.at[g, chip], row, 2 * owner_of(kind, item) + core,
        )

    def arrived(g, kind, source):
        return remote(
            held[kind].at[g, 0, 0], line[kind].at[g, source],
            r.line_send.at[g, 0], r.line_recv.at[g, source], row, 2 * source + core,
        )

    def across(mask):
        there = row
        for bit in range(steps):
            if (mask >> bit) & 1:
                there = flip(there, bit)
        return there

    def spread_out(g, kind, step):
        return remote(
            fin[kind].at[g, row], fin[kind].at[g, row],
            r.spread_send.at[g, step - 1], r.spread_recv.at[g, step - 1], across(step), col,
        )

    def each_owner(body):
        for kind, here, item in ((0, is_query, chip), (1, is_out, chip - (chips - half))):
            @pl.when(here)
            def _(kind=kind, item=item):
                body(kind, item)

    def line_finish(g):
        def body(kind, item):
            total = None
            for source in range(kind, chips, 2) if g == paired else range(chips):
                @pl.when(chip != source)
                def _(source=source):
                    arrived(g, kind, source).wait_recv()

                value = line[kind][g, source].astype(F32)
                total = value if total is None else total + value
            fin[kind][g, row] = total.astype(BF16)
            for step in range(rows_n - 1, 0, -1):
                spread_out(g, kind, step).start()

        each_owner(body)

    def place_final(g):
        def body(kind, item):
            for step in range(1, rows_n):
                spread_out(g, kind, step).wait()
            for part in range(rows_n):
                value = fin[kind][g, part].astype(F32)
                if kind == 0:
                    size = channels // rows_n
                    r.grad_weights[part * size : (part + 1) * size, g * part_lanes : (g + 1) * part_lanes] = value
                else:
                    size = WIDE // rows_n
                    k = (part * size) // part_lanes
                    at = k * shard + g * part_lanes + part * size - k * part_lanes
                    r.grad_weights[at : at + size] = value

        each_owner(body)

    go_copy.wait()
    hidden_copy.wait()
    for g in range(groups):
        attend(g)
    for step in range(1, cols_n):
        block(step).start()
    for g in range(groups):
        terms(g)
        if g == paired:
            pair_start()
        else:
            halve_start(g)

    @pl.loop(0, 2)
    def _(at):
        rows = chunk_of(at)
        value = contract(grad_query[rows], r.w_query_v[...], 1, 1) + grad_out[rows].astype(F32)
        pad2[pl.ds(1 + at * (height // 2), height // 2)] = value.reshape(height // 2, width, channels)

    halve_finish(0, 0)

    for at in range(height):
        for which, value in enumerate((pad2[at + 1, 0:1], pad2[at + 1, width - 1 : width])):
            r.stage1[which, at : at + 1] = value
    r.tap_terms[...] = jnp.zeros_like(r.tap_terms)

    @pl.loop(0, parts)
    def _(part):
        lanes = lanes_of(part)
        sums = [jnp.zeros((8, LANES), F32) for _ in range(9)]
        for at in range(height):
            value = pad2[at + 1, :, lanes]
            shifted = [from_right(value, 0.0), value, from_left(value, 0.0)]
            for a in range(3):
                x = pad1[at + a, :, lanes]
                for b in range(3):
                    sums[3 * a + b] = sums[3 * a + b] + (shifted[b] * x).reshape(width // 8, 8, LANES).sum(axis=0)
        for i in range(9):
            total = sums[i].sum(axis=0, keepdims=True)
            if i % 3 != 1:
                which = 0 if i % 3 == 0 else 1
                product = r.stage1[which, :, lanes] * r.side1[which, i // 3 : i // 3 + height, lanes]
                total = total + product.sum(axis=0, keepdims=True)
            r.tap_terms[i : i + 1, lanes] = total

    totals = r.blocks[col].astype(F32)
    for step in range(1, cols_n):
        block(step).wait()
        totals = totals + r.blocks_in[step - 1].astype(F32)
    high, low = split(totals)
    tot_all = r.tot_all
    tot_all[col] = high

    def tot(target):
        return remote(
            tot_all.at[col], tot_all.at[col], r.tot_send.at[target - quarter], r.tot_recv.at[col], row, target
        )

    def tot_from(source):
        return remote(
            tot_all.at[source], tot_all.at[source], r.tot_send.at[0], r.tot_recv.at[source], row, source
        )

    for target in range(quarter, 3 * quarter):
        @pl.when(col != target)
        def _(target=target):
            tot(target).start()

    both_parts = jnp.concatenate([high, low], axis=0)
    by_key = contract(both_parts, r.w_key_v[...], 1, 1)
    by_value = contract(both_parts, r.w_value_v[...], 1, 1)
    grad_normed = by_key[:own] + by_key[2 * own : 3 * own] + by_value[own : 2 * own] + by_value[3 * own :]
    grad_pooled = (
        grad_normed
        - jnp.mean(grad_normed, axis=-1, keepdims=True)
        - standard * jnp.mean(grad_normed * standard, axis=-1, keepdims=True)
    ) * (inverse / (POOL * POOL))
    r.grad_pooled[...] = grad_pooled
    narrow = channels // cols_n
    for i in range(9):
        r.tap_terms[i : i + 1] = r.tap_terms[i : i + 1] + (r.windows[i] * grad_pooled).sum(axis=0, keepdims=True)
    for at in range(cols_n):
        r.tap_out[at] = r.tap_terms[:, at * narrow : (at + 1) * narrow].astype(BF16)

    def tap_first(step):
        return remote(
            r.tap_out.at[col_mate(step)], r.tap_in.at[step - 1],
            r.tap_send1.at[step - 1], r.tap_recv1.at[step - 1], row, col_mate(step),
        )

    def tap_second(step):
        return remote(
            r.tap_out2, r.tap_in2.at[step - 1], r.tap_send2.at[step - 1], r.tap_recv2.at[step - 1], row_mate(step), col
        )

    for step in range(1, cols_n):
        tap_first(step).start()

    for g in range(1, groups - 1):
        halve_finish(g, 0)
    pair_finish()

    @pl.loop(0, parts)
    def _(part):
        lanes = lanes_of(part)
        for cell_row in range(height // POOL):
            over = jnp.concatenate(
                [
                    jnp.broadcast_to(r.grad_pooled[at : at + 1, lanes], (POOL, LANES))
                    for at in range(cell_row * per_row, (cell_row + 1) * per_row)
                ],
                axis=0,
            )
            for at in range(cell_row * POOL, (cell_row + 1) * POOL):
                value = pad2[at + 1, :, lanes] + over
                pad2[at + 1, :, lanes] = value
                if at == 0 or at == height - 1:
                    r.rows_out2[0 if at == 0 else 1, :, lanes] = value.astype(BF16)

    pack_edges(halo2, lambda at: pad2[at + 1, 0:1], lambda at: pad2[at + 1, width - 1 : width])
    send_halo(halo2, range(8))

    for g in range(groups - 1):
        for step in range(1, steps):
            halve_finish(g, step)
    halve_finish(paired, 0)

    @pl.when(is_cells)
    def _():
        for step in range(1, cols_n):
            tot_from(col_mate(step)).wait_recv()
        is_key = col < 2 * quarter
        sides = []
        for at in range(cols_n):
            value = tot_all[at].astype(F32)
            sides.append(jnp.where(is_key, value[:own], value[own:]))
        value = jnp.concatenate(sides, axis=0)
        mine = value[:, :shard]
        for k in range(1, quarter):
            mine = jnp.where(lax.rem(col, quarter) == k, value[:, k * shard : (k + 1) * shard], mine)
        r.side_all[row] = mine.astype(BF16)
        for step in range(1, rows_n):
            pass_on(r.side_all, 1, step).start()

    tap_total = r.tap_out[col].astype(F32)
    for step in range(1, cols_n):
        tap_first(step).wait()
        tap_total = tap_total + r.tap_in[step - 1].astype(F32)
    r.tap_out2[...] = tap_total.astype(BF16)
    for step in range(1, rows_n):
        tap_second(step).start()

    for step in range(1, steps):
        halve_finish(groups - 1, step)
    for g in range(groups):
        line_finish(g)
    wait_halo(halo2)
    take_halo(halo2)

    @pl.loop(0, parts)
    def _(part):
        lanes = lanes_of(part)
        w = weights_of(lanes)
        short = [jnp.broadcast_to(taps[i : i + 1, lanes], (height, LANES)) for i in range(9)]
        for which in range(2):
            total = jnp.zeros((height, LANES), F32)
            for a in range(3):
                total = total + short[3 * a + 2 - 2 * which] * r.side2[which, 2 - a : 2 - a + height, lanes]
            r.edge_sum[which, :, lanes] = total
        for at in range(height):
            x = [pad2[at + 2 - a, :, lanes] for a in range(3)]
            sums = [w[b] * x[0] + w[3 + b] * x[1] + w[6 + b] * x[2] for b in range(3)]
            total = (
                sums[1]
                + from_right(sums[0], r.edge_sum[1, at : at + 1, lanes])
                + from_left(sums[2], r.edge_sum[0, at : at + 1, lanes])
            )
            r.grad_image[at, :, lanes] = total.astype(BF16)

    @pl.when(is_cells)
    def _():
        for at, ref in enumerate((r.key_all, r.side_all)):
            for step in range(1, rows_n):
                pass_on(ref, at, step).wait()
        keys = r.key_all[...].reshape(rows_n * cells_n, channels)
        sides = r.side_all[...].reshape(rows_n * cells_n, shard)
        r.grad_weights[...] = contract(keys, sides, 0, 0)

    tap_total = r.tap_out2[...].astype(F32)
    for step in range(1, rows_n):
        tap_second(step).wait()
        tap_total = tap_total + r.tap_in2[step - 1].astype(F32)
    r.grad_conv[...] = tap_total[:9]

    for g in range(groups):
        place_final(g)

    for target in range(quarter, 3 * quarter):
        @pl.when(col != target)
        def _(target=target):
            tot(target).wait_send()
    def drain(g, kind):
        for item in range(half):
            @pl.when(chip != owner_of(kind, item))
            def _(item=item):
                along(g, kind, item).wait_send()

    for g in range(groups):
        kept(g, partial(drain, g))


def store_kernel(count, *refs):
    copies = [pltpu.make_async_copy(refs[at], refs[count + at], refs[2 * count].at[at]) for at in range(count)]
    for copy in copies:
        copy.start()
    for copy in copies:
        copy.wait()


def on_device(image, conv_taps, w_query, w_key, w_value, w_out, grad_out):
    rows_n, cols_n = lax.axis_size("row"), lax.axis_size("col")
    height, width, channels = image.shape
    tokens = height * width
    own = (height // POOL) * (width // POOL)
    cells_n = cols_n * own
    chips, quarter = cols_n // 2, cols_n // 4
    half = quarter // 2
    shard = 4 * channels // cols_n
    groups = channels // WIDE
    part_lanes = shard // groups
    steps = bits_of(rows_n)
    part_q, part_o = (channels // rows_n, part_lanes), (WIDE // rows_n, shard)
    operands = dict(
        image=image, grad_out=grad_out.reshape(tokens, channels), taps=conv_taps,
        w_query=w_query, w_key=w_key, w_value=w_value, w_out=w_out,
    )
    outputs = dict(
        grad_image=(image.shape, BF16),
        grad_weights=((channels, shard), F32),
        grad_conv=((9, channels // cols_n), F32),
    )
    square = ((channels, channels), BF16)
    flat = ((tokens, channels), BF16)
    edge_cols, edge_rows = ((2, height, channels), BF16), ((2, width, channels), BF16)
    corner = ((4, 8, channels), F32)
    scratch = dict(
        image_v=(image.shape, BF16), grad_out_v=flat, taps_v=(conv_taps.shape, F32),
        w_query_v=square, w_key_v=square, w_value_v=square, w_out_v=square,
        pad1=((height + 2, width, channels), F32), pad2=((height + 2, width, channels), F32),
        stage1=((2, height, channels), F32), stage2=((2, height, channels), F32),
        side1=((2, height + 8, channels), F32), side2=((2, height + 8, channels), F32),
        edge_sum=((2, height, channels), F32), mixed=((height, width, channels), F32),
        windows=((9, own, channels), F32),
        rows_out2=edge_rows,
        hidden=flat, query=flat, dout=flat, grad_query=flat, hidden_in=flat,
        go_split=((2, half, tokens, shard), BF16), go_in=((half, tokens, shard), BF16),
        gq_split=((groups, 2, half, tokens, part_lanes), BF16), gq_in=((groups, half, tokens, part_lanes), BF16),
        att=((groups, tokens, WIDE), BF16), att_in=((groups, tokens, WIDE), BF16),
        pooled=((own, channels), F32), grad_pooled=((own, channels), F32),
        cellbuf=((cols_n, own, channels), BF16),
        keys=((cells_n, channels), BF16), values=((cells_n, channels), BF16),
        key_all=((rows_n, cells_n, channels), BF16), side_all=((rows_n, cells_n, shard), BF16),
        blocks=((cols_n, 2 * own, channels), BF16), blocks_in=((cols_n - 1, 2 * own, channels), BF16),
        tot_all=((cols_n, 2 * own, channels), BF16),
        cols_out1=edge_cols, cols_in1=edge_cols, rows_in1=edge_rows, corners_in1=corner, corners_out1=corner,
        cols_out2=edge_cols, cols_in2=edge_cols, rows_in2=edge_rows, corners_in2=corner, corners_out2=corner,
        terms_q=((groups, half, rows_n) + part_q, BF16), terms_o=((groups, half, rows_n) + part_o, BF16),
        landed_q=((groups, half, rows_n - 1) + part_q, BF16), landed_o=((groups, half, rows_n - 1) + part_o, BF16),
        held_q=((groups, half, rows_n // 2) + part_q, BF16), held_o=((groups, half, rows_n // 2) + part_o, BF16),
        line_q=((groups, chips) + part_q, BF16), line_o=((groups, chips) + part_o, BF16),
        fin_q=((groups, rows_n) + part_q, BF16), fin_o=((groups, rows_n) + part_o, BF16),
        pair_q=((half, rows_n) + part_q, BF16), pair_o=((half, rows_n) + part_o, BF16),
        tap_terms=((16, channels), F32),
        tap_out=((cols_n, 16, channels // cols_n), BF16), tap_in=((cols_n - 1, 16, channels // cols_n), BF16),
        tap_out2=((16, channels // cols_n), BF16), tap_in2=((rows_n - 1, 16, channels // cols_n), BF16),
    )
    sems = dict(
        loaded=(7,), pair_sems=(2,),
        halo_send1=(8,), halo_recv1=(8,), halo_send2=(8,), halo_recv2=(8,),
        mate_send=(2 + 2 * groups,), mate_recv=(2 + 2 * groups,),
        cell_send=(cols_n - 1,), cell_recv=(cols_n - 1,),
        block_send=(cols_n - 1,), block_recv=(cols_n - 1,),
        tot_send=(2 * quarter,), tot_recv=(cols_n,),
        half_send=(groups, 2 * half, steps), half_recv=(groups, 2 * half, steps),
        line_send=(groups, 2 * half), line_recv=(groups, chips),
        spread_send=(groups, rows_n - 1), spread_recv=(groups, rows_n - 1),
        tap_send1=(cols_n - 1,), tap_recv1=(cols_n - 1,),
        tap_send2=(rows_n - 1,), tap_recv2=(rows_n - 1,),
        pass_send=(2, rows_n - 1), pass_recv=(2, rows_n - 1),
    )
    names = list(operands) + list(outputs) + list(scratch) + list(sems)
    made = pl.pallas_call(
        partial(block_kernel, rows_n, cols_n, names),
        out_shape=[pltpu.VMEM(*spec) for spec in outputs.values()],
        in_specs=[HBM] * len(operands),
        out_specs=[pl.BlockSpec(memory_space=pltpu.VMEM)] * len(outputs),
        scratch_shapes=[pltpu.VMEM(*spec) for spec in scratch.values()]
        + [pltpu.SemaphoreType.DMA(spec) for spec in sems.values()],
        compiler_params=pltpu.CompilerParams(
            collective_id=0, has_side_effects=True, vmem_limit_bytes=48 * 2**20
        ),
    )(*[pltpu.with_memory_space_constraint(value, pltpu.HBM) for value in operands.values()])
    return tuple(
        pl.pallas_call(
            partial(store_kernel, len(outputs)),
            out_shape=[pltpu.HBM(*spec) for spec in outputs.values()],
            in_specs=[pl.BlockSpec(memory_space=pltpu.VMEM)] * len(outputs),
            out_specs=[HBM] * len(outputs),
            scratch_shapes=[pltpu.SemaphoreType.DMA((len(outputs),))],
        )(*[pltpu.with_memory_space_constraint(value, pltpu.VMEM) for value in made])
    )


def solution(mesh):
    return jax.shard_map(
        on_device,
        mesh=mesh,
        in_specs=(P("row", "col", None), P(), P(), P(), P(), P(), P("row", "col", None)),
        out_specs=(P("row", "col", None), P(None, "col"), P(None, "col")),
        check_vma=False,
    )
```
